32 devices in a mesh: tx: 4 (over z), ty: 8 (over y, x, core).
Axes of the slice: x: 2, y: 2, z: 4, core: 2. Of those that a mesh axis runs over, the one named last changes fastest.
Arguments:
- source: bfloat16 [256, 512, 2, 128], P('tx', 'ty'), may hold values from -6 to 6
- guess: bfloat16 [256, 512, 2, 128], P('tx', 'ty'), may hold values from -6 to 6
- coefficient: float32 [256, 512], P('tx', 'ty'), may hold values from 0.25 to 2.5
- leaf_map: float32 [4, 8, 2, 256, 256], P('tx', 'ty'), may hold values from -0.9 to 0.9, as said below
- body_map: bfloat16 [4, 8, 2, 256, 4096], P('tx', 'ty'), may hold values from -0.013671875 to 0.013671875
Outputs:
- top_map: float32 [4, 8, 2, 64, 768], P('tx', 'ty')
- top_outgoing: float32 [4, 8, 2, 64, 128], P('tx', 'ty')
The draws below stay inside these ranges and needn't reach their ends.
Inputs may be any that keep to these rules, and one draw needn't show every extreme that they name: `leaf_map`: as a complex matrix, each tile's map has spectral norm at most 0.9.
All inputs are finite; a program needn't handle non-finite values.
Results may differ from the reference program's by a relative error of at most 0.0029.
Values may be sent and summed in bfloat16 or wider, within the bound.
A program may use at most 64 MiB of HBM per device.

```python
import math
from functools import partial
import jax
import jax.numpy as jnp
import numpy as np
from jax import lax

TILE = 64
RHS = 128
TILE_ROWS = 4
TILE_COLS = 8
NX = 256
NY = 512
ORDER = 256
CELLS = 4096


def cayley_embedded(real_draw, imag_draw):
    skew_real = (real_draw - real_draw.T) / math.sqrt(2.0)
    sym_imag = (imag_draw + imag_draw.T) / math.sqrt(2.0)
    upper_half = jnp.concatenate([skew_real, -sym_imag], axis=1)
    lower_half = jnp.concatenate([sym_imag, skew_real], axis=1)
    embedded = jnp.concatenate([upper_half, lower_half], axis=0)
    identity = jnp.eye(embedded.shape[0], dtype=jnp.float32)
    return jnp.linalg.solve(identity + embedded, identity - embedded)


def leaf_tile(tile_key):
    sub_keys = jax.random.split(tile_key, 2)
    random_parts = jax.random.normal(sub_keys[0], (4, ORDER, ORDER), jnp.float32)
    lowest = 0.8
    side_index = jnp.arange(ORDER) // TILE
    same_side = (side_index[:, None] == side_index[None, :]).astype(jnp.float32)
    other_side = 1.0 - same_side
    side_scale = 2.0 / math.sqrt(TILE)
    mix_scale = 0.32 / math.sqrt(ORDER)
    side_unitary = cayley_embedded(random_parts[0] * same_side * side_scale, random_parts[1] * same_side * side_scale)
    mix_unitary = cayley_embedded(random_parts[2] * other_side * mix_scale, random_parts[3] * other_side * mix_scale)
    unitary = jnp.dot(side_unitary, mix_unitary, precision=lax.Precision.HIGHEST, preferred_element_type=jnp.float32)
    column_scales = jnp.exp(jax.random.uniform(sub_keys[1], (ORDER,), jnp.float32, math.log(lowest), math.log(0.9)))
    real_block = unitary[:ORDER, :ORDER] * column_scales[None, :]
    imag_block = unitary[ORDER:, :ORDER] * column_scales[None, :]
    return jnp.stack([real_block, imag_block])


def draw_leaf_map(key, part):
    tile_keys = jax.random.split(key, TILE_ROWS * TILE_COLS)
    tiles_all = lax.map(leaf_tile, tile_keys)
    return tiles_all.reshape(TILE_ROWS, TILE_COLS, 2, ORDER, ORDER)


def level_of(stream_key, shape, cuts, low, largest):
    loudness = 1.0
    for position, parts in cuts:
        steps = jax.random.uniform(jax.random.fold_in(jax.random.fold_in(stream_key, 6), position), (parts,), jnp.float32, low / len(cuts), largest / len(cuts))
        loudness = loudness * jnp.repeat(jnp.exp(steps), shape[position] // parts).reshape((-1,) + (1,) * (len(shape) - 1 - position))
    return loudness


def noise(rng, shape, scale, most, shards=(), kind=jnp.bfloat16):
    loudness = level_of(rng, shape, shards, -0.22, 0.18) if shards else 1.0
    entries = jax.random.normal(rng, shape, jnp.float32) * scale * loudness
    return jnp.minimum(jnp.maximum(entries, -most), most).astype(kind)


def setup_inputs(seed: int = 0) -> dict:
    key_of = jax.random.split(jax.random.key(seed), 6)
    source = noise(key_of[0], (NX, NY, 2, RHS), 1.0, 6.0, ((0, 4), (1, 8)))
    guess = noise(key_of[1], (NX, NY, 2, RHS), 1.0, 6.0, ((0, 4), (1, 8)))
    coefficient = jnp.clip(jnp.exp(math.log(2.5) - 2.3025851 * jax.random.uniform(key_of[2], (NX, NY), jnp.float32) ** level_of(key_of[2], (NX, NY), ((0, 4), (1, 8)), -0.2, 0.2)), 0.25, 2.5)
    leaf_map = draw_leaf_map(jax.random.fold_in(key_of[5], 71), 0)
    body_map = noise(key_of[4], (TILE_ROWS, TILE_COLS, 2, ORDER, CELLS), (50 * CELLS) ** -0.5, 0.013671875, ((0, 4), (1, 8)))
    return {"source": source, "guess": guess, "coefficient": coefficient, "leaf_map": leaf_map, "body_map": body_map}


DAMPING = 0.5
SQUARINGS = 8

def matmul_high(left, right):
    return jnp.dot(left.astype(jnp.float32), right.astype(jnp.float32), precision=lax.Precision.HIGHEST, preferred_element_type=jnp.float32)

def complex_dot(left, right):
    real_part = matmul_high(left[0], right[0]) - matmul_high(left[1], right[1])
    imag_part = matmul_high(left[0], right[1]) + matmul_high(left[1], right[0])
    return jnp.stack([real_part, imag_part])

def complex_solve(reflect, right_part):
    answer = right_part
    power = reflect
    for step_num in range(SQUARINGS):
        answer = answer + complex_dot(power, answer)
        if step_num + 1 < SQUARINGS:
            power = complex_dot(power, power)
    return answer

def side_pieces(side_counts, tile_len):
    pieces = []
    offset = 0
    for segments in side_counts:
        pieces.append((offset, segments * tile_len))
        offset = offset + segments * tile_len
    return pieces

def select_pieces(matrix, pieces, axis_num):
    return jnp.concatenate([lax.slice_in_dim(matrix, begin_at, begin_at + length, axis=axis_num) for begin_at, length in pieces], axis=axis_num)

def face_sides(vertical):
    if vertical:
        return (2, 0)
    return (1, 3)

def interface_coef(face_a, face_out_a, face_b, face_out_b, ext_a, ext_b, side_a, side_b):
    cross_a = select_pieces(face_a, ext_a, 2)
    inner_a = select_pieces(face_a, [side_a], 2)
    cross_b = select_pieces(face_b, ext_b, 2)
    inner_b = select_pieces(face_b, [side_b], 2)
    product = complex_dot(inner_b, inner_a)
    right_part = jnp.concatenate([complex_dot(inner_b, cross_a), -cross_b, complex_dot(inner_b, face_out_a) - face_out_b], axis=2)
    return complex_solve(product, right_part)

def interface_wave(face_a, face_out_a, coeffs, ext_a, side_a, len_b):
    cross_a = select_pieces(face_a, ext_a, 2)
    inner_a = select_pieces(face_a, [side_a], 2)
    filler = jnp.zeros((2, cross_a.shape[1], len_b), jnp.float32)
    return -jnp.concatenate([cross_a, filler, face_out_a], axis=2) - complex_dot(inner_a, coeffs)

def rows_first(rows_map, rows_out, coeffs, ext_a, side_a, len_b):
    local_part = select_pieces(rows_map, ext_a, 2)
    across = select_pieces(rows_map, [side_a], 2)
    filler = jnp.zeros((2, rows_map.shape[1], len_b), jnp.float32)
    return complex_dot(across, coeffs) + jnp.concatenate([local_part, filler, rows_out], axis=2)

def rows_second(rows_map, rows_out, waves, ext_b, side_b, len_a):
    local_part = select_pieces(rows_map, ext_b, 2)
    across = select_pieces(rows_map, [side_b], 2)
    filler = jnp.zeros((2, rows_map.shape[1], len_a), jnp.float32)
    return complex_dot(across, waves) + jnp.concatenate([filler, local_part, rows_out], axis=2)

def merge_pair(map_a, out_a, map_b, out_b, side_counts, vertical, tile_len):
    pieces = side_pieces(side_counts, tile_len)
    idx_a, idx_b = face_sides(vertical)
    ext_a = [pieces[k] for k in range(4) if k != idx_a]
    ext_b = [pieces[k] for k in range(4) if k != idx_b]
    len_a = sum((p[1] for p in ext_a))
    len_b = sum((p[1] for p in ext_b))
    face_a = select_pieces(map_a, [pieces[idx_a]], 1)
    face_out_a = select_pieces(out_a, [pieces[idx_a]], 1)
    face_b = select_pieces(map_b, [pieces[idx_b]], 1)
    face_out_b = select_pieces(out_b, [pieces[idx_b]], 1)
    coeffs = interface_coef(face_a, face_out_a, face_b, face_out_b, ext_a, ext_b, pieces[idx_a], pieces[idx_b])
    waves = interface_wave(face_a, face_out_a, coeffs, ext_a, pieces[idx_a], len_b)
    upper_rows = rows_first(select_pieces(map_a, ext_a, 1), select_pieces(out_a, ext_a, 1), coeffs, ext_a, pieces[idx_a], len_b)
    lower_rows = rows_second(select_pieces(map_b, ext_b, 1), select_pieces(out_b, ext_b, 1), waves, ext_b, pieces[idx_b], len_a)
    joined = jnp.concatenate([upper_rows, lower_rows], axis=1)
    map_cols = len_a + len_b
    return (joined[:, :, :map_cols], joined[:, :, map_cols:])

def canonical_order(side_counts, vertical, tile_len):
    south_len, east_len, north_len, west_len = [c * tile_len for c in side_counts]
    if vertical:
        lengths = [south_len, east_len, west_len, east_len, north_len, west_len]
        sequence = [0, 1, 3, 4, 2, 5]
        merged = (side_counts[0], 2 * side_counts[1], side_counts[2], 2 * side_counts[3])
    else:
        lengths = [south_len, north_len, west_len, south_len, east_len, north_len]
        sequence = [0, 3, 4, 1, 5, 2]
        merged = (2 * side_counts[0], side_counts[1], 2 * side_counts[2], side_counts[3])
    begins = [sum(lengths[:k]) for k in range(6)]
    return ([(begins[k], lengths[k]) for k in sequence], merged)

def reorder_box(box_map, box_out, pieces):
    return (select_pieces(select_pieces(box_map, pieces, 1), pieces, 2), select_pieces(box_out, pieces, 1))

def residual_of(source, padded, coefficient):
    center = padded[1:-1, 1:-1]
    beside_all = padded[2:, 1:-1] + padded[:-2, 1:-1] + padded[1:-1, 2:] + padded[1:-1, :-2]
    wave_term = coefficient[:, :, None]
    diagonal_term = 4.0 - wave_term
    real_part = diagonal_term * center[:, :, 0] + wave_term * DAMPING * center[:, :, 1] - beside_all[:, :, 0]
    imag_part = diagonal_term * center[:, :, 1] - wave_term * DAMPING * center[:, :, 0] - beside_all[:, :, 1]
    applied = jnp.stack([real_part, imag_part], axis=2)
    return (source.astype(jnp.float32) - applied).astype(jnp.bfloat16)

def leaf_rows(inputs):
    maps_row, cells_row = inputs
    products = jnp.einsum('tack,tkbr->tabcr', maps_row.astype(jnp.float32), cells_row.astype(jnp.float32), precision=lax.Precision.HIGHEST)
    real_part = products[:, 0, 0] - products[:, 1, 1]
    imag_part = products[:, 0, 1] + products[:, 1, 0]
    return jnp.stack([real_part, imag_part], axis=1)

def flatten_grid(matrix):
    return matrix.reshape((-1,) + matrix.shape[2:])

def spread_rows(top_arrays):
    seg_table = np.array([[0, 1], [5, 3], [10, 6], [8, 9]])
    blocks = top_arrays.reshape(top_arrays.shape[:3] + (12, TILE, top_arrays.shape[-1]))
    chosen = blocks[:, :, :, seg_table]
    return chosen.transpose(0, 3, 1, 4, 2, 5, 6).reshape(TILE_ROWS, TILE_COLS, 2, TILE, top_arrays.shape[-1])

def reference(source, guess, coefficient, leaf_map, body_map):
    padded = jnp.pad(guess.astype(jnp.float32), ((1, 1), (1, 1), (0, 0), (0, 0)))
    residual = residual_of(source, padded, coefficient)
    cells = residual.reshape(TILE_ROWS, TILE, TILE_COLS, TILE, 2, RHS).transpose(0, 2, 1, 3, 4, 5).reshape(TILE_ROWS, TILE_COLS, CELLS, 2, RHS)
    outgoing = lax.map(leaf_rows, (body_map, cells))
    maps = leaf_map
    side_counts = (1, 1, 1, 1)
    for layer_idx in range(3):
        vertical = layer_idx % 2 == 0
        if vertical:
            map_a, map_b = (maps[0::2], maps[1::2])
            out_a, out_b = (outgoing[0::2], outgoing[1::2])
        else:
            map_a, map_b = (maps[:, 0::2], maps[:, 1::2])
            out_a, out_b = (outgoing[:, 0::2], outgoing[:, 1::2])
        grid_shape = map_a.shape[:2]
        merge_fn = partial(merge_pair, side_counts=side_counts, vertical=vertical, tile_len=TILE)
        new_maps, new_out = jax.vmap(merge_fn)(flatten_grid(map_a), flatten_grid(out_a), flatten_grid(map_b), flatten_grid(out_b))
        if layer_idx < 2:
            pieces, side_counts = canonical_order(side_counts, vertical, TILE)
            new_maps, new_out = jax.vmap(partial(reorder_box, pieces=pieces))(new_maps, new_out)
        maps = new_maps.reshape(grid_shape + new_maps.shape[1:])
        outgoing = new_out.reshape(grid_shape + new_out.shape[1:])
    return (spread_rows(maps), spread_rows(outgoing))
```

```python
import functools

import jax
import jax.numpy as jnp
from jax import lax
from jax.experimental import pallas as pl
from jax.experimental.pallas import tpu as pltpu
from jax.sharding import PartitionSpec as P

DAMPING = 0.5
DOUBLINGS = 7
LANES = 128
MESH = pl.DeviceIdType.MESH
F32 = jnp.float32
BF16 = jnp.bfloat16


def split(x):
    high = x.astype(BF16)
    return high, (x - high.astype(F32)).astype(BF16)


def dot1(a, b):
    return jnp.dot(a, b, preferred_element_type=F32)


def dot3(a, b):
    a_high, a_low = split(a)
    b_high, b_low = split(b)
    return dot1(a_high, b_high) + (dot1(a_high, b_low) + dot1(a_low, b_high))


def tile(x, k):
    return x[:, k * LANES : (k + 1) * LANES]


def cols(parts):
    return jnp.concatenate(parts, axis=1)


def rows(parts):
    return jnp.concatenate(parts, axis=0)


def half_roll(x):
    return pltpu.roll(x, LANES // 2, 1)


def low_lanes(shape):
    return lax.broadcasted_iota(jnp.int32, shape, 1) < LANES // 2


def low_low(a, b):
    return jnp.where(low_lanes(a.shape), a, half_roll(b))


def high_high(a, b):
    return jnp.where(low_lanes(a.shape), half_roll(a), b)


def embed(re, im):
    return rows([cols([re, -im]), cols([im, re])])


def embed_low(re, im):
    return rows([low_low(re, -im), low_low(im, re)])


def identity(n):
    return (
        lax.broadcasted_iota(jnp.int32, (n, n), 0) == lax.broadcasted_iota(jnp.int32, (n, n), 1)
    ).astype(F32)


def inverse(power, pow_ref, inv_ref):
    n = power.shape[0]
    pow_ref[:n, :n] = dot3(power, power)
    inv_ref[:n, :n] = identity(n) + power

    def body(k, carry):
        now, total = pow_ref[:n, :n], inv_ref[:n, :n]
        both = dot3(now, cols([now, total]))
        pow_ref[:n, :n] = both[:, :n]
        inv_ref[:n, :n] = total + both[:, n:]
        return carry

    lax.fori_loop(0, DOUBLINGS - 2, body, 0)
    total = inv_ref[:n, :n]
    return total + dot3(pow_ref[:n, :n], total)


def swapped_view(block):
    return cols([half_roll(tile(block, 0)), tile(block, 2), tile(block, 1), tile(block, 3)])


def merge_kernel(
    map_ref, out_ref, top_ref, top_out_ref,
    own0, face1, face2, x1, x2, face3, pow_ref, inv_ref,
    send1, recv1, send2, recv2, send3, recv3,
):
    p = lax.axis_index("tx")
    q = lax.axis_index("ty")
    p_low = lax.rem(p, 4)
    p_odd = lax.rem(p, 2)
    q_odd = lax.rem(q, 2)
    vertical = p + 1 - 2 * p_odd
    beside = q + 1 - 2 * q_odd
    inner = (p_low == 1) | (p_low == 2)
    inner_num = jnp.where(inner, 1, 0)
    lower = p_low < 2
    facing = p + 3 - 2 * p_low
    side = map_ref.shape[1] // 4

    barrier = pltpu.get_barrier_semaphore()
    for target in ((vertical, q), (p, beside)):
        pl.semaphore_signal(barrier, inc=1, device_id=target, device_id_type=MESH)

    @pl.when(inner)
    def _():
        pl.semaphore_signal(barrier, inc=1, device_id=(facing, q), device_id_type=MESH)

    pl.semaphore_wait(barrier, 2 + inner_num)

    def remote(src, dst, send, recv, target):
        return pltpu.make_async_remote_copy(
            src_ref=src, dst_ref=dst, send_sem=send, recv_sem=recv,
            device_id=target, device_id_type=MESH,
        )

    starts = [
        jnp.where(p_odd == 1, 0, 2 * side),
        jnp.where(q_odd == 1, 3 * side, side),
        jnp.where(p_odd == 1, 2 * side, 0),
        jnp.where(q_odd == 1, side, 3 * side),
    ]
    lane = lax.broadcasted_iota(jnp.int32, (side, LANES), 1)
    vert_swap = jnp.where(p_odd == 1, 0, 1)
    cross = jnp.where(lane < LANES // 2, vert_swap, q_odd) == 1
    for k in range(4):
        begin = pl.multiple_of(starts[k], side)
        for c in range(2):
            left = map_ref[c, pl.ds(begin, side), :LANES]
            right = map_ref[c, pl.ds(begin, side), LANES:]
            own0[c, k * side : (k + 1) * side, :LANES] = jnp.where(cross, right, left)
            own0[c, k * side : (k + 1) * side, LANES : 2 * LANES] = jnp.where(cross, left, right)
            own0[c, k * side : (k + 1) * side, 2 * LANES :] = out_ref[c, pl.ds(begin, side), :]

    first = remote(own0.at[:, :side], face1, send1, recv1, (vertical, q))
    first.start()
    first.wait()

    mine = own0[0, :side], own0[1, :side]
    theirs = face1[0], face1[1]
    across = embed_low(tile(theirs[0], 0), tile(theirs[1], 0))
    stacked = rows(theirs)
    product = dot3(across, rows(mine))
    turned = tile(product, 0)
    inv = inverse(embed_low(turned[:side], turned[side:]), pow_ref, inv_ref)
    right_part = cols([
        jnp.where(low_lanes(turned.shape), half_roll(turned), -tile(stacked, 0)),
        tile(product, 1),
        -tile(stacked, 1),
        tile(product, 2) - tile(stacked, 2),
    ])
    wave = dot3(inv, right_part)
    rest = own0[0, side:], own0[1, side:]
    gain = dot3(embed_low(tile(rest[0], 0), tile(rest[1], 0)), wave)
    count = 3 * side
    for c in range(2):
        part = gain[c * count : (c + 1) * count]
        first_tile = tile(rest[c], 0)
        x1[c, :, :LANES] = tile(part, 0) + jnp.where(
            low_lanes(first_tile.shape), half_roll(first_tile), 0.0
        )
        x1[c, :, LANES : 2 * LANES] = tile(part, 1) + tile(rest[c], 1)
        x1[c, :, 2 * LANES : 3 * LANES] = tile(part, 2)
        x1[c, :, 3 * LANES :] = tile(part, 3) + tile(rest[c], 2)

    to_vert = remote(x1.at[:, :side], face2.at[0], send2.at[0], recv2.at[0], (vertical, q))
    to_side = remote(x1.at[:, :side], face2.at[1], send2.at[1], recv2.at[1], (p, beside))
    to_vert.start()
    to_side.start()
    to_vert.wait_recv()
    relay = remote(face2.at[0], face2.at[2], send2.at[2], recv2.at[2], (p, beside))
    relay.start()
    to_side.wait_recv()
    relay.wait_recv()
    to_vert.wait_send()
    to_side.wait_send()
    relay.wait_send()
    mine = [rows([x1[c, :side], swapped_view(face2[0, c])]) for c in range(2)]
    theirs = [rows([face2[1, c], swapped_view(face2[2, c])]) for c in range(2)]
    stacked = rows(theirs)
    product = dot3(embed(tile(theirs[0], 0), tile(theirs[1], 0)), rows(mine))
    turned = tile(product, 0)
    inv = inverse(embed(turned[: 2 * side], turned[2 * side :]), pow_ref, inv_ref)
    right_part = cols([
        tile(product, 1),
        tile(product, 2),
        -tile(stacked, 1),
        -tile(stacked, 2),
        tile(product, 3) - tile(stacked, 3),
    ])
    wave = dot3(inv, right_part)
    rest = x1[0, side:], x1[1, side:]
    gain = dot3(embed(tile(rest[0], 0), tile(rest[1], 0)), wave)
    count = 2 * side
    for c in range(2):
        part = gain[c * count : (c + 1) * count]
        t_own = tile(part, 0) + tile(rest[c], 1)
        t_vert = tile(part, 1) + tile(rest[c], 2)
        t_side = tile(part, 2)
        t_diag = tile(part, 3)
        own_0 = jnp.where(q_odd == 1, t_side, t_own)
        own_1 = jnp.where(q_odd == 1, t_own, t_side)
        vert_0 = jnp.where(q_odd == 1, t_diag, t_vert)
        vert_1 = jnp.where(q_odd == 1, t_vert, t_diag)
        in_0 = jnp.where(inner, own_0, vert_0)
        in_1 = jnp.where(inner, own_1, vert_1)
        out_0 = jnp.where(inner, vert_0, own_0)
        out_1 = jnp.where(inner, vert_1, own_1)
        x2[c, :, :LANES] = low_low(in_0, in_1)
        x2[c, :, LANES : 2 * LANES] = low_low(out_0, out_1)
        x2[c, :, 2 * LANES : 3 * LANES] = jnp.where(
            lower, high_high(out_1, in_1), high_high(in_1, out_1)
        )
        x2[c, :, 3 * LANES : 4 * LANES] = jnp.where(
            lower, high_high(out_0, in_0), high_high(in_0, out_0)
        )
        x2[c, :, 4 * LANES :] = tile(part, 4) + tile(rest[c], 3)

    def send_face(src, box, slot, target):
        return remote(src, face3.at[box, q_odd], send3.at[slot], recv3.at[slot], target)

    up_own = lambda: send_face(x2.at[:, :side], 0, 0, (vertical, q))
    up_other = lambda: send_face(face3.at[1, q_odd], 1, 1, (vertical, q))
    over = lambda: send_face(x2.at[:, :side], 1, 2, (facing, q))

    @pl.when(inner)
    def _():
        over().start()
        up_own().start()
        send_face(x2.at[:, :side], 0, 3, (p, beside)).start()
        face3[0, q_odd] = x2[:, :side]
        over().wait_recv()
        up_other().start()
        side_other = send_face(face3.at[1, q_odd], 1, 4, (p, beside))
        side_other.start()
        over().wait_send()
        up_own().wait_send()
        up_other().wait_send()
        send_face(x2.at[:, :side], 0, 3, (p, beside)).wait()
        side_other.wait()

    @pl.when(jnp.logical_not(inner))
    def _():
        up_own().wait_recv()
        side_own = send_face(face3.at[0, q_odd], 0, 3, (p, beside))
        side_own.start()
        up_other().wait_recv()
        side_other = send_face(face3.at[1, q_odd], 1, 4, (p, beside))
        side_other.start()
        side_own.wait()
        side_other.wait()

    mine = [rows([face3[0, 0, c], face3[0, 1, c]]) for c in range(2)]
    theirs = [rows([face3[1, 0, c], face3[1, 1, c]]) for c in range(2)]
    stacked = rows(theirs)
    product = dot3(embed(tile(theirs[0], 0), tile(theirs[1], 0)), rows(mine))
    turned = tile(product, 0)
    inv = inverse(embed(turned[: 2 * side], turned[2 * side :]), pow_ref, inv_ref)
    right_part = cols([
        tile(product, 1),
        tile(product, 2),
        tile(product, 3),
        -tile(stacked, 1),
        -tile(stacked, 2),
        -tile(stacked, 3),
        tile(product, 4) - tile(stacked, 4),
    ])
    wave = dot3(inv, right_part)
    begin = pl.multiple_of(inner_num * side, side)
    rest = x2[0, pl.ds(begin, side)], x2[1, pl.ds(begin, side)]
    gain = dot3(embed(tile(rest[0], 0), tile(rest[1], 0)), wave)
    for c in range(2):
        part = gain[c * side : (c + 1) * side]
        own = [tile(part, k) + tile(rest[c], k + 1) for k in range(3)]
        other = [tile(part, k + 3) for k in range(3)]
        low = [jnp.where(lower, a, b) for a, b in zip(own, other)]
        up = [jnp.where(lower, b, a) for a, b in zip(own, other)]
        for k, value in enumerate([low[0], low[1], low[2], up[1], up[0], up[2]]):
            top_ref[c, :, k * LANES : (k + 1) * LANES] = value
        top_out_ref[c] = tile(part, 6) + tile(rest[c], 4)


def merge_tree(leaf_map, outgoing):
    order = leaf_map.shape[1]
    side = order // 4
    rhs = outgoing.shape[2]
    vmem = pl.BlockSpec(memory_space=pltpu.VMEM)
    dma = pltpu.SemaphoreType.DMA
    return pl.pallas_call(
        merge_kernel,
        name="merge_tree",
        out_shape=(
            jax.ShapeDtypeStruct((2, side, 12 * side), F32),
            jax.ShapeDtypeStruct((2, side, rhs), F32),
        ),
        in_specs=[vmem, vmem],
        out_specs=(vmem, vmem),
        scratch_shapes=[
            pltpu.VMEM((2, order, order + rhs), F32),
            pltpu.VMEM((2, side, order + rhs), F32),
            pltpu.VMEM((3, 2, side, 6 * side + rhs), F32),
            pltpu.VMEM((2, 3 * side, 6 * side + rhs), F32),
            pltpu.VMEM((2, 2 * side, 8 * side + rhs), F32),
            pltpu.VMEM((2, 2, 2, side, 8 * side + rhs), F32),
            pltpu.VMEM((order, order), F32),
            pltpu.VMEM((order, order), F32),
            dma, dma, dma((3,)), dma((3,)), dma((5,)), dma((5,)),
        ],
        compiler_params=pltpu.CompilerParams(
            collective_id=0, has_side_effects=True, vmem_limit_bytes=48 * 1024 * 1024
        ),
    )(leaf_map, outgoing)


def padded_2(cells, sides, width):
    for axis, dim in sides:
        count = lax.axis_size(axis)
        ends = count - 1
        head = lax.slice_in_dim(cells, 0, width, axis=dim)
        tail = lax.slice_in_dim(cells, cells.shape[dim] - width, cells.shape[dim], axis=dim)
        cells = jnp.concatenate(
            [
                lax.ppermute(tail, axis, [(i, (i + 1) % count) for i in range(ends)]),
                cells,
                lax.ppermute(head, axis, [((i + 1) % count, i) for i in range(ends)]),
            ],
            axis=dim,
        )
    return cells


def residual_of(source, padded, coefficient):
    center = padded[1:-1, 1:-1]
    beside_all = padded[2:, 1:-1] + padded[:-2, 1:-1] + padded[1:-1, 2:] + padded[1:-1, :-2]
    wave_term = coefficient[:, :, None]
    diagonal_term = 4.0 - wave_term
    real_part = (
        diagonal_term * center[:, :, 0]
        + wave_term * DAMPING * center[:, :, 1]
        - beside_all[:, :, 0]
    )
    imag_part = (
        diagonal_term * center[:, :, 1]
        - wave_term * DAMPING * center[:, :, 0]
        - beside_all[:, :, 1]
    )
    applied = jnp.stack([real_part, imag_part], axis=2)
    return (source.astype(jnp.float32) - applied).astype(jnp.bfloat16)


def on_device(source, guess, coefficient, leaf_map, body_map):
    padded = padded_2(guess, (("tx", 0), ("ty", 1)), 1).astype(jnp.float32)
    residual = residual_of(source, padded, coefficient)
    tile_len = guess.shape[0]
    cells = residual.reshape(tile_len * tile_len, 2, guess.shape[3])
    products = jnp.einsum(
        "ack,kbr->abcr", body_map[0, 0], cells, preferred_element_type=jnp.float32
    )
    outgoing = jnp.stack([products[0, 0] - products[1, 1], products[0, 1] + products[1, 0]])
    own_map, own_out = merge_tree(leaf_map[0, 0], outgoing)
    return (own_map[None, None], own_out[None, None])


def solution(mesh):
    placed = (
        P("tx", "ty", None, None),
        P("tx", "ty", None, None),
        P("tx", "ty"),
        P("tx", "ty", None, None, None),
        P("tx", "ty", None, None, None),
    )
    return jax.shard_map(
        on_device,
        mesh=mesh,
        in_specs=placed,
        out_specs=(P("tx", "ty", None, None, None), P("tx", "ty", None, None, None)),
        check_vma=False,
    )
```

```python
import functools

import jax
import jax.numpy as jnp
from jax import lax
from jax.experimental import pallas as pl
from jax.experimental.pallas import tpu as pltpu
from jax.sharding import PartitionSpec as P

DAMPING = 0.5
DOUBLINGS = 7
LANES = 128
MESH = pl.DeviceIdType.MESH
F32 = jnp.float32
BF16 = jnp.bfloat16
WIRE = F32


def split(x):
    high = x.astype(BF16)
    return high, (x - high.astype(F32)).astype(BF16)


def dot1(a, b):
    return jnp.dot(a, b, preferred_element_type=F32)


def dot3(a, b):
    a_high, a_low = split(a)
    b_high, b_low = split(b)
    return dot1(a_high, b_high) + (dot1(a_high, b_low) + dot1(a_low, b_high))


def tile(x, k):
    return x[:, k * LANES : (k + 1) * LANES]


def cols(parts):
    return jnp.concatenate(parts, axis=1)


def rows(parts):
    return jnp.concatenate(parts, axis=0)


def half_roll(x):
    return pltpu.roll(x, LANES // 2, 1)


def low_lanes(shape):
    return lax.broadcasted_iota(jnp.int32, shape, 1) < LANES // 2


def low_low(a, b):
    return jnp.where(low_lanes(a.shape), a, half_roll(b))


def high_high(a, b):
    return jnp.where(low_lanes(a.shape), half_roll(a), b)


def embed(re, im):
    return rows([cols([re, -im]), cols([im, re])])


def embed_low(re, im):
    return rows([low_low(re, -im), low_low(im, re)])


def identity(n):
    return (
        lax.broadcasted_iota(jnp.int32, (n, n), 0) == lax.broadcasted_iota(jnp.int32, (n, n), 1)
    ).astype(F32)


def inverse(power, pow_ref, inv_ref):
    n = power.shape[0]
    pow_ref[:n, :n] = dot3(power, power)
    inv_ref[:n, :n] = identity(n) + power

    def body(k, carry):
        now, total = pow_ref[:n, :n], inv_ref[:n, :n]
        both = dot3(now, cols([now, total]))
        pow_ref[:n, :n] = both[:, :n]
        inv_ref[:n, :n] = total + both[:, n:]
        return carry

    lax.fori_loop(0, DOUBLINGS - 2, body, 0)
    total = inv_ref[:n, :n]
    return total + dot3(pow_ref[:n, :n], total)


def swapped_view(block):
    return cols([half_roll(tile(block, 0)), tile(block, 2), tile(block, 1)])


def tree_kernel(
    guess_ref, guess_rows_ref, source_ref, coef_ref, map_ref, body_ref, top_ref, top_out_ref,
    guess_v, source_v, body_v, edge_v, beside_v, coef_v, plain, field, load_a, load_b,
    m0, h0, m1, h1, m2, h2, out2, out3,
    face1, face1h, face2, face2h, face3, face3h, pow_ref, inv_ref, cross1, cross2, cross3,
    local_sem, halo_send, halo_recv, send1, recv1, send2, recv2, send3, recv3,
):
    p = lax.axis_index("tx")
    q = lax.axis_index("ty")
    p_ends = lax.axis_size("tx") - 1
    q_ends = lax.axis_size("ty") - 1
    p_low = lax.rem(p, 4)
    p_odd = lax.rem(p, 2)
    q_odd = lax.rem(q, 2)
    vertical = p + 1 - 2 * p_odd
    beside = q + 1 - 2 * q_odd
    inner = (p_low == 1) | (p_low == 2)
    inner_num = jnp.where(inner, 1, 0)
    lower = p_low < 2
    facing = p + 3 - 2 * p_low
    side = map_ref.shape[1] // 4
    length = guess_ref.shape[0]
    last = length - 1

    def remote(src, dst, send, recv, target):
        return pltpu.make_async_remote_copy(
            src_ref=src, dst_ref=dst, send_sem=send, recv_sem=recv,
            device_id=target, device_id_type=MESH,
        )

    halos = [
        (p < p_ends, p > 0, (p + 1, q),
         lambda: remote(guess_rows_ref.at[last], edge_v.at[0], halo_send.at[0], halo_recv.at[0], (p + 1, q))),
        (p > 0, p < p_ends, (p - 1, q),
         lambda: remote(guess_rows_ref.at[0], edge_v.at[1], halo_send.at[1], halo_recv.at[1], (p - 1, q))),
        (q < q_ends, q > 0, (p, q + 1),
         lambda: remote(guess_ref.at[:, last], beside_v.at[0], halo_send.at[2], halo_recv.at[2], (p, q + 1))),
        (q > 0, q < q_ends, (p, q - 1),
         lambda: remote(guess_ref.at[:, 0], beside_v.at[1], halo_send.at[3], halo_recv.at[3], (p, q - 1))),
    ]
    locals_ = [
        pltpu.make_async_copy(guess_rows_ref, guess_v, local_sem.at[0]),
        pltpu.make_async_copy(source_ref, source_v, local_sem.at[1]),
        pltpu.make_async_copy(body_ref, body_v, local_sem.at[2]),
    ]
    for copy in locals_:
        copy.start()
    barrier = pltpu.get_barrier_semaphore()
    arrivals = 0
    for exists, _, target, _ in halos:
        arrivals = arrivals + jnp.where(exists, 1, 0)

        @pl.when(exists)
        def _():
            pl.semaphore_signal(barrier, inc=1, device_id=target, device_id_type=MESH)

    pl.semaphore_wait(barrier, arrivals)
    for exists, _, _, copy in halos:

        @pl.when(exists)
        def _():
            copy().start()

    starts = [
        jnp.where(p_odd == 1, 0, 2 * side),
        jnp.where(q_odd == 1, 3 * side, side),
        jnp.where(p_odd == 1, 2 * side, 0),
        jnp.where(q_odd == 1, side, 3 * side),
    ]
    starts = [pl.multiple_of(begin, side) for begin in starts]
    lane = lax.broadcasted_iota(jnp.int32, (side, LANES), 1)
    vert_swap = jnp.where(p_odd == 1, 0, 1)
    cross = jnp.where(lane < LANES // 2, vert_swap, q_odd) == 1

    first = remote(m0.at[:, :side], face1, send1.at[0], recv1.at[0], (vertical, q))
    for k in range(4):
        for c in range(2):
            left = map_ref[c, pl.ds(starts[k], side), :LANES]
            right = map_ref[c, pl.ds(starts[k], side), LANES:]
            m0[c, k * side : (k + 1) * side, :LANES] = jnp.where(cross, right, left)
            m0[c, k * side : (k + 1) * side, LANES:] = jnp.where(cross, left, right)
        if k == 0:
            first.start()

    pad = 8
    locals_[0].wait()

    def apart(k, carry):
        plain[...] = guess_v[k].astype(F32)
        for c in range(2):
            field[c, k + 1, pad : pad + length] = plain[pl.ds(c, length, 2), :]
        return carry

    lax.fori_loop(0, length, apart, 0)
    coef_v[...] = jnp.zeros_like(coef_v)
    coef_v[:length, :length] = coef_ref[...]
    coef_t = jnp.transpose(coef_v[...])[:length]
    coef_v[:length] = coef_t
    for num, (exists, arrives, _, copy) in enumerate(halos):

        @pl.when(arrives)
        def _():
            copy().wait_recv()
            if num < 2:
                plain[...] = edge_v[num].astype(F32)
                for c in range(2):
                    field[c, (0, length + 1)[num], pad : pad + length] = plain[pl.ds(c, length, 2), :]
            else:
                strip = beside_v[num - 2].astype(F32)
                at = (pad - 1, pad + length)[num - 2]
                for c in range(2):
                    field[c, 1 : length + 1, at : at + 1] = strip[:, c : c + 1]

        @pl.when(jnp.logical_not(arrives))
        def _():
            for c in range(2):
                if num < 2:
                    field[c, (0, length + 1)[num], pad : pad + length] = jnp.zeros((length, LANES), F32)
                else:
                    at = (pad - 1, pad + length)[num - 2]
                    field[c, 1 : length + 1, at : at + 1] = jnp.zeros((length, 1, LANES), F32)

    locals_[1].wait()

    def residual_row(k, carry):
        plain[...] = source_v[k].astype(F32)
        wave_term = jnp.broadcast_to(
            pltpu.roll(coef_v[:length], lax.rem(LANES - k, LANES), 1)[:, :1], (length, LANES)
        )
        diagonal_term = 4.0 - wave_term
        damp = wave_term * DAMPING
        center = [field[c, k + 1, pad : pad + length] for c in range(2)]
        around = [
            field[c, k + 2, pad : pad + length]
            + field[c, k, pad : pad + length]
            + field[c, k + 1, pad + 1 : pad + 1 + length]
            + field[c, k + 1, pad - 1 : pad - 1 + length]
            for c in range(2)
        ]
        real_part = diagonal_term * center[0] + damp * center[1] - around[0]
        imag_part = diagonal_term * center[1] - damp * center[0] - around[1]
        real = (plain[pl.ds(0, length, 2), :] - real_part).astype(BF16)
        imag = (plain[pl.ds(1, length, 2), :] - imag_part).astype(BF16)
        at = pl.ds(pl.multiple_of(k * length, length), length)
        load_a[at, :LANES] = real
        load_a[at, LANES:] = imag
        load_b[at, :LANES] = -imag
        load_b[at, LANES:] = real
        return carry

    lax.fori_loop(0, length, residual_row, 0)

    first.wait()
    mine = rows([m0[0, :side], m0[1, :side]])
    theirs = rows([face1[0], face1[1]])
    across = embed_low(theirs[:side, :LANES], theirs[side:, :LANES])
    cross1[0] = across
    product = dot3(across, mine)
    turned = tile(product, 0)
    inv = inverse(embed_low(turned[:side], turned[side:]), pow_ref, inv_ref)
    cross1[1] = inv
    wave = dot3(inv, cols([
        jnp.where(low_lanes(turned.shape), half_roll(turned), -tile(theirs, 0)),
        tile(product, 1),
        -tile(theirs, 1),
    ]))
    rest = m0[0, side:], m0[1, side:]
    gain = dot3(embed_low(tile(rest[0], 0), tile(rest[1], 0)), wave)
    count = 3 * side
    for c in range(2):
        part = gain[c * count : (c + 1) * count]
        first_tile = tile(rest[c], 0)
        m1[c, :, :LANES] = tile(part, 0) + jnp.where(
            low_lanes(first_tile.shape), half_roll(first_tile), 0.0
        )
        m1[c, :, LANES : 2 * LANES] = tile(part, 1) + tile(rest[c], 1)
        m1[c, :, 2 * LANES :] = tile(part, 2)
    out2[...] = m1[:, :side].astype(WIRE)

    def exchange(src, face, kind):
        return (
            remote(src, face.at[0], send2.at[kind, 0], recv2.at[kind, 0], (vertical, q)),
            remote(src, face.at[1], send2.at[kind, 1], recv2.at[kind, 1], (p, beside)),
            remote(face.at[0], face.at[2], send2.at[kind, 2], recv2.at[kind, 2], (p, beside)),
        )

    maps2 = exchange(out2, face2, 0)
    maps2[0].start()
    maps2[1].start()

    locals_[2].wait()
    leaf = dot1(body_v[0], load_a[...]) + dot1(body_v[1], load_b[...])
    inv_ref[...] = leaf
    for k in range(4):
        for c in range(2):
            h0[c, k * side : (k + 1) * side] = inv_ref[
                pl.ds(starts[k], side), c * LANES : (c + 1) * LANES
            ]
    first_h = remote(h0.at[:, :side], face1h, send1.at[1], recv1.at[1], (vertical, q))
    first_h.start()
    maps2[0].wait_recv()
    maps2[2].start()
    first_h.wait()
    wave = dot3(
        cross1[1],
        dot3(cross1[0], rows([h0[0, :side], h0[1, :side]])) - rows([face1h[0], face1h[1]]),
    )
    rest = m0[0, side:], m0[1, side:]
    gain = dot3(embed_low(tile(rest[0], 0), tile(rest[1], 0)), wave)
    for c in range(2):
        h1[c] = gain[c * count : (c + 1) * count] + h0[c, side:]
    data2 = exchange(h1.at[:, :side], face2h, 1)
    data2[0].start()
    data2[1].start()

    maps2[1].wait_recv()
    maps2[2].wait_recv()
    for copy in maps2:
        copy.wait_send()
    mine = rows([
        x for c in range(2) for x in (m1[c, :side], swapped_view(face2[0, c].astype(F32)))
    ])
    theirs = rows([
        x
        for c in range(2)
        for x in (face2[1, c].astype(F32), swapped_view(face2[2, c].astype(F32)))
    ])
    across = embed(theirs[: 2 * side, :LANES], theirs[2 * side :, :LANES])
    cross2[0] = across
    product = dot3(across, mine)
    turned = tile(product, 0)
    inv = inverse(embed(turned[: 2 * side], turned[2 * side :]), pow_ref, inv_ref)
    cross2[1] = inv
    wave = dot3(inv, cols([
        tile(product, 1), tile(product, 2), -tile(theirs, 1), -tile(theirs, 2),
    ]))
    rest = m1[0, side:], m1[1, side:]
    gain = dot3(embed(tile(rest[0], 0), tile(rest[1], 0)), wave)
    count2 = 2 * side
    for c in range(2):
        part = gain[c * count2 : (c + 1) * count2]
        t_own = tile(part, 0) + tile(rest[c], 1)
        t_vert = tile(part, 1) + tile(rest[c], 2)
        t_side = tile(part, 2)
        t_diag = tile(part, 3)
        own_0 = jnp.where(q_odd == 1, t_side, t_own)
        own_1 = jnp.where(q_odd == 1, t_own, t_side)
        vert_0 = jnp.where(q_odd == 1, t_diag, t_vert)
        vert_1 = jnp.where(q_odd == 1, t_vert, t_diag)
        in_0 = jnp.where(inner, own_0, vert_0)
        in_1 = jnp.where(inner, own_1, vert_1)
        out_0 = jnp.where(inner, vert_0, own_0)
        out_1 = jnp.where(inner, vert_1, own_1)
        m2[c, :, :LANES] = low_low(in_0, in_1)
        m2[c, :, LANES : 2 * LANES] = low_low(out_0, out_1)
        m2[c, :, 2 * LANES : 3 * LANES] = jnp.where(
            lower, high_high(out_1, in_1), high_high(in_1, out_1)
        )
        m2[c, :, 3 * LANES :] = jnp.where(
            lower, high_high(out_0, in_0), high_high(in_0, out_0)
        )
    out3[...] = m2[:, :side].astype(WIRE)

    def last_copies(src, face, kind):
        def send(source, box, slot, target):
            return remote(
                source, face.at[box, q_odd], send3.at[kind, slot], recv3.at[kind, slot], target
            )

        return (
            lambda: send(src, 0, 0, (vertical, q)),
            lambda: send(face.at[1, q_odd], 1, 1, (vertical, q)),
            lambda: send(src, 1, 2, (facing, q)),
            lambda: send(src, 0, 3, (p, beside)),
            lambda: send(face.at[0, q_odd], 0, 3, (p, beside)),
            lambda: send(face.at[1, q_odd], 1, 4, (p, beside)),
        )

    def last_start(copies, src, face):
        up_own, up_other, over, side_own, side_relay, side_other = copies

        @pl.when(inner)
        def _():
            over().start()
            up_own().start()
            side_own().start()
            face[0, q_odd] = src[:, :side]

    def last_relay(copies):
        up_own, up_other, over, side_own, side_relay, side_other = copies

        @pl.when(inner)
        def _():
            over().wait_recv()
            up_other().start()
            side_other().start()

        @pl.when(jnp.logical_not(inner))
        def _():
            up_own().wait_recv()
            side_relay().start()
            up_other().wait_recv()
            side_other().start()

    def last_wait(copies):
        up_own, up_other, over, side_own, side_relay, side_other = copies
        side_own().wait_recv()
        side_other().wait_recv()

    def last_drain(copies):
        up_own, up_other, over, side_own, side_relay, side_other = copies
        side_own().wait_send()
        side_other().wait_send()

        @pl.when(inner)
        def _():
            over().wait_send()
            up_own().wait_send()
            up_other().wait_send()

    maps3 = last_copies(out3, face3, 0)
    last_start(maps3, out3, face3)

    data2[0].wait_recv()
    data2[2].start()
    data2[1].wait_recv()
    data2[2].wait_recv()
    mine = rows([x for c in range(2) for x in (h1[c, :side], face2h[0, c])])
    theirs = rows([x for c in range(2) for x in (face2h[1, c], face2h[2, c])])
    wave = dot3(cross2[1], dot3(cross2[0], mine) - theirs)
    rest = m1[0, side:], m1[1, side:]
    gain = dot3(embed(tile(rest[0], 0), tile(rest[1], 0)), wave)
    for c in range(2):
        h2[c] = gain[c * count2 : (c + 1) * count2] + h1[c, side:]
    data3 = last_copies(h2.at[:, :side], face3h, 1)
    last_start(data3, h2, face3h)
    last_relay(maps3)
    last_relay(data3)

    last_wait(maps3)
    mine = rows([face3[0, j, c].astype(F32) for c in range(2) for j in range(2)])
    theirs = rows([face3[1, j, c].astype(F32) for c in range(2) for j in range(2)])
    across = embed(theirs[: 2 * side, :LANES], theirs[2 * side :, :LANES])
    product = dot3(across, mine)
    turned = tile(product, 0)
    inv = inverse(embed(turned[: 2 * side], turned[2 * side :]), pow_ref, inv_ref)
    begin = pl.multiple_of(inner_num * side, side)
    rest = m2[0, pl.ds(begin, side)], m2[1, pl.ds(begin, side)]
    out_gain = dot3(embed(tile(rest[0], 0), tile(rest[1], 0)), inv)
    cross3[0] = across
    cross3[1, : 2 * side] = out_gain
    gain = dot3(out_gain, cols(
        [tile(product, k) for k in range(1, 4)] + [-tile(theirs, k) for k in range(1, 4)]
    ))
    for c in range(2):
        part = gain[c * side : (c + 1) * side]
        own = [tile(part, k) + tile(rest[c], k + 1) for k in range(3)]
        other = [tile(part, k + 3) for k in range(3)]
        low = [jnp.where(lower, a, b) for a, b in zip(own, other)]
        up = [jnp.where(lower, b, a) for a, b in zip(own, other)]
        for k, value in enumerate([low[0], low[1], low[2], up[1], up[0], up[2]]):
            top_ref[c, :, k * LANES : (k + 1) * LANES] = value
    last_wait(data3)
    mine = rows([face3h[0, j, c] for c in range(2) for j in range(2)])
    theirs = rows([face3h[1, j, c] for c in range(2) for j in range(2)])
    gain = dot3(cross3[1, : 2 * side], dot3(cross3[0], mine) - theirs)
    for c in range(2):
        top_out_ref[c] = gain[c * side : (c + 1) * side] + h2[c, pl.ds(begin, side)]
    for copy in data2:
        copy.wait_send()
    last_drain(maps3)
    last_drain(data3)
    for exists, _, _, copy in halos:

        @pl.when(exists)
        def _():
            copy().wait_send()


def on_device(source, guess, coefficient, leaf_map, body_map):
    length, width, _, rhs = guess.shape
    order = leaf_map.shape[3]
    side = order // 4
    vmem = pl.BlockSpec(memory_space=pltpu.VMEM)
    hbm = pl.BlockSpec(memory_space=pl.ANY)
    dma = pltpu.SemaphoreType.DMA
    rows_of = lambda x: x.reshape(length, 2 * width, rhs)
    own_map, own_out = pl.pallas_call(
        tree_kernel,
        name="build_tree",
        out_shape=(
            jax.ShapeDtypeStruct((2, side, 12 * side), F32),
            jax.ShapeDtypeStruct((2, side, rhs), F32),
        ),
        in_specs=[hbm, hbm, hbm, vmem, vmem, hbm],
        out_specs=(vmem, vmem),
        scratch_shapes=[
            pltpu.VMEM((length, 2 * width, rhs), BF16),
            pltpu.VMEM((length, 2 * width, rhs), BF16),
            pltpu.VMEM((2, order, length * width), BF16),
            pltpu.VMEM((2, 2 * width, rhs), BF16),
            pltpu.VMEM((2, length, 2, rhs), BF16),
            pltpu.VMEM((LANES, LANES), F32),
            pltpu.VMEM((2 * width, rhs), F32),
            pltpu.VMEM((2, length + 2, width + 16, rhs), F32),
            pltpu.VMEM((length * width, 2 * rhs), BF16),
            pltpu.VMEM((length * width, 2 * rhs), BF16),
            pltpu.VMEM((2, order, order), F32),
            pltpu.VMEM((2, order, rhs), F32),
            pltpu.VMEM((2, 3 * side, 6 * side), F32),
            pltpu.VMEM((2, 3 * side, rhs), F32),
            pltpu.VMEM((2, 2 * side, 8 * side), F32),
            pltpu.VMEM((2, 2 * side, rhs), F32),
            pltpu.VMEM((2, side, 6 * side), WIRE),
            pltpu.VMEM((2, side, 8 * side), WIRE),
            pltpu.VMEM((2, side, order), F32),
            pltpu.VMEM((2, side, rhs), F32),
            pltpu.VMEM((3, 2, side, 6 * side), WIRE),
            pltpu.VMEM((3, 2, side, rhs), F32),
            pltpu.VMEM((2, 2, 2, side, 8 * side), WIRE),
            pltpu.VMEM((2, 2, 2, side, rhs), F32),
            pltpu.VMEM((order, order), F32),
            pltpu.VMEM((order, order), F32),
            pltpu.VMEM((2, 2 * side, 2 * side), F32),
            pltpu.VMEM((2, order, order), F32),
            pltpu.VMEM((2, order, order), F32),
            dma((3,)), dma((4,)), dma((4,)), dma((2,)), dma((2,)),
            dma((2, 3)), dma((2, 3)), dma((2, 5)), dma((2, 5)),
        ],
        compiler_params=pltpu.CompilerParams(
            collective_id=0, has_side_effects=True, vmem_limit_bytes=56 * 1024 * 1024
        ),
    )(guess, rows_of(guess), rows_of(source), coefficient, leaf_map[0, 0], body_map[0, 0])
    return (own_map[None, None], own_out[None, None])


def solution(mesh):
    placed = (
        P("tx", "ty", None, None),
        P("tx", "ty", None, None),
        P("tx", "ty"),
        P("tx", "ty", None, None, None),
        P("tx", "ty", None, None, None),
    )
    return jax.shard_map(
        on_device,
        mesh=mesh,
        in_specs=placed,
        out_specs=(P("tx", "ty", None, None, None), P("tx", "ty", None, None, None)),
        check_vma=False,
    )
```

```python
import functools

import jax
import jax.numpy as jnp
from jax import lax
from jax.experimental import pallas as pl
from jax.experimental.pallas import tpu as pltpu
from jax.sharding import PartitionSpec as P

DAMPING = 0.5
DOUBLINGS = 7
LANES = 128
MESH = pl.DeviceIdType.MESH
F32 = jnp.float32
BF16 = jnp.bfloat16
WIRE = BF16
UNROLL = 4


def split(x):
    high = x.astype(BF16)
    return high, (x - high.astype(F32)).astype(BF16)


def dot1(a, b):
    return jnp.dot(a, b, preferred_element_type=F32)


def dot3(a, b):
    a_high, a_low = split(a)
    b_high, b_low = split(b)
    return dot1(a_high, b_high) + (dot1(a_high, b_low) + dot1(a_low, b_high))


def tile(x, k):
    return x[:, k * LANES : (k + 1) * LANES]


def cols(parts):
    return jnp.concatenate(parts, axis=1)


def rows(parts):
    return jnp.concatenate(parts, axis=0)


def half_roll(x):
    return pltpu.roll(x, LANES // 2, 1)


def low_lanes(shape):
    return lax.broadcasted_iota(jnp.int32, shape, 1) < LANES // 2


def low_low(a, b):
    return jnp.where(low_lanes(a.shape), a, half_roll(b))


def high_high(a, b):
    return jnp.where(low_lanes(a.shape), half_roll(a), b)


def embed(re, im):
    return rows([cols([re, -im]), cols([im, re])])


def embed_low(re, im):
    return rows([low_low(re, -im), low_low(im, re)])


def identity(n):
    return (
        lax.broadcasted_iota(jnp.int32, (n, n), 0) == lax.broadcasted_iota(jnp.int32, (n, n), 1)
    ).astype(F32)


def inverse(power, pow_ref, inv_ref):
    n = power.shape[0]
    pow_ref[:n, :n] = dot3(power, power)
    inv_ref[:n, :n] = identity(n) + power

    def body(k, carry):
        now, total = pow_ref[:n, :n], inv_ref[:n, :n]
        both = dot3(now, cols([now, total]))
        pow_ref[:n, :n] = both[:, :n]
        inv_ref[:n, :n] = total + both[:, n:]
        return carry

    lax.fori_loop(0, DOUBLINGS - 2, body, 0)
    total = inv_ref[:n, :n]
    return total + dot3(pow_ref[:n, :n], total)


def swapped_view(block):
    return cols([half_roll(tile(block, 0)), tile(block, 2), tile(block, 1)])


def tree_kernel(
    guess_ref, guess_rows_ref, source_ref, coef_ref, map_ref, body_ref, top_ref, top_out_ref,
    guess_v, source_v, body_v, edge_v, beside_v, coef_v, plain, field, load_a, load_b,
    m0, h0, m1, h1, m2, h2, out2, out3,
    face1, face1h, face2, face2h, face3, face3h, pow_ref, inv_ref, cross1, cross2, cross3,
    local_sem, halo_send, halo_recv, send1, recv1, send2, recv2, send3, recv3,
):
    p = lax.axis_index("tx")
    q = lax.axis_index("ty")
    p_ends = lax.axis_size("tx") - 1
    q_ends = lax.axis_size("ty") - 1
    p_low = lax.rem(p, 4)
    p_odd = lax.rem(p, 2)
    q_odd = lax.rem(q, 2)
    vertical = p + 1 - 2 * p_odd
    beside = q + 1 - 2 * q_odd
    inner = (p_low == 1) | (p_low == 2)
    inner_num = jnp.where(inner, 1, 0)
    lower = p_low < 2
    facing = p + 3 - 2 * p_low
    side = map_ref.shape[1] // 4
    length = guess_ref.shape[0]
    last = length - 1

    def remote(src, dst, send, recv, target):
        return pltpu.make_async_remote_copy(
            src_ref=src, dst_ref=dst, send_sem=send, recv_sem=recv,
            device_id=target, device_id_type=MESH,
        )

    halos = [
        (p < p_ends, p > 0, (p + 1, q),
         lambda: remote(guess_rows_ref.at[last], edge_v.at[0], halo_send.at[0], halo_recv.at[0], (p + 1, q))),
        (p > 0, p < p_ends, (p - 1, q),
         lambda: remote(guess_rows_ref.at[0], edge_v.at[1], halo_send.at[1], halo_recv.at[1], (p - 1, q))),
        (q < q_ends, q > 0, (p, q + 1),
         lambda: remote(guess_ref.at[:, last], beside_v.at[0], halo_send.at[2], halo_recv.at[2], (p, q + 1))),
        (q > 0, q < q_ends, (p, q - 1),
         lambda: remote(guess_ref.at[:, 0], beside_v.at[1], halo_send.at[3], halo_recv.at[3], (p, q - 1))),
    ]
    locals_ = [
        pltpu.make_async_copy(guess_rows_ref, guess_v, local_sem.at[0]),
        pltpu.make_async_copy(source_ref, source_v, local_sem.at[1]),
        pltpu.make_async_copy(body_ref, body_v, local_sem.at[2]),
    ]
    for copy in locals_:
        copy.start()
    barrier = pltpu.get_barrier_semaphore()
    arrivals = 0
    for exists, _, target, _ in halos:
        arrivals = arrivals + jnp.where(exists, 1, 0)

        @pl.when(exists)
        def _():
            pl.semaphore_signal(barrier, inc=1, device_id=target, device_id_type=MESH)

    pl.semaphore_wait(barrier, arrivals)
    for exists, _, _, copy in halos:

        @pl.when(exists)
        def _():
            copy().start()

    starts = [
        jnp.where(p_odd == 1, 0, 2 * side),
        jnp.where(q_odd == 1, 3 * side, side),
        jnp.where(p_odd == 1, 2 * side, 0),
        jnp.where(q_odd == 1, side, 3 * side),
    ]
    starts = [pl.multiple_of(begin, side) for begin in starts]
    lane = lax.broadcasted_iota(jnp.int32, (side, LANES), 1)
    vert_swap = jnp.where(p_odd == 1, 0, 1)
    cross = jnp.where(lane < LANES // 2, vert_swap, q_odd) == 1

    first = remote(m0.at[:, :side], face1, send1.at[0], recv1.at[0], (vertical, q))
    for k in range(4):
        for c in range(2):
            left = map_ref[c, pl.ds(starts[k], side), :LANES]
            right = map_ref[c, pl.ds(starts[k], side), LANES:]
            m0[c, k * side : (k + 1) * side, :LANES] = jnp.where(cross, right, left)
            m0[c, k * side : (k + 1) * side, LANES:] = jnp.where(cross, left, right)
        if k == 0:
            first.start()

    pad = 8
    locals_[0].wait()

    def apart(k, carry):
        slot = lax.rem(k, UNROLL)
        plain[slot] = guess_v[k].astype(F32)
        for c in range(2):
            field[c, k + 1, pad : pad + length] = plain[slot, pl.ds(c, length, 2), :]
        return carry

    lax.fori_loop(0, length, apart, 0, unroll=UNROLL)
    coef_v[...] = jnp.zeros_like(coef_v)
    coef_v[:length, :length] = coef_ref[...]
    coef_t = jnp.transpose(coef_v[...])[:length]
    coef_v[:length] = coef_t
    first.wait()
    mine = rows([m0[0, :side], m0[1, :side]])
    theirs = rows([face1[0], face1[1]])
    across = embed_low(theirs[:side, :LANES], theirs[side:, :LANES])
    cross1[0] = across
    product = dot3(across, mine)
    turned = tile(product, 0)
    inv = inverse(embed_low(turned[:side], turned[side:]), pow_ref, inv_ref)
    cross1[1] = inv
    wave = dot3(inv, cols([
        jnp.where(low_lanes(turned.shape), half_roll(turned), -tile(theirs, 0)),
        tile(product, 1),
        -tile(theirs, 1),
    ]))
    rest = m0[0, side:], m0[1, side:]
    gain = dot3(embed_low(tile(rest[0], 0), tile(rest[1], 0)), wave)
    count = 3 * side
    for c in range(2):
        part = gain[c * count : (c + 1) * count]
        first_tile = tile(rest[c], 0)
        m1[c, :, :LANES] = tile(part, 0) + jnp.where(
            low_lanes(first_tile.shape), half_roll(first_tile), 0.0
        )
        m1[c, :, LANES : 2 * LANES] = tile(part, 1) + tile(rest[c], 1)
        m1[c, :, 2 * LANES :] = tile(part, 2)
    out2[...] = m1[:, :side].astype(WIRE)

    def exchange(src, face, kind):
        return (
            remote(src, face.at[0], send2.at[kind, 0], recv2.at[kind, 0], (vertical, q)),
            remote(src, face.at[1], send2.at[kind, 1], recv2.at[kind, 1], (p, beside)),
            remote(face.at[0], face.at[2], send2.at[kind, 2], recv2.at[kind, 2], (p, beside)),
        )

    maps2 = exchange(out2, face2, 0)
    maps2[0].start()
    maps2[1].start()

    for num, (exists, arrives, _, copy) in enumerate(halos):

        @pl.when(arrives)
        def _():
            copy().wait_recv()
            if num < 2:
                plain[0] = edge_v[num].astype(F32)
                for c in range(2):
                    field[c, (0, length + 1)[num], pad : pad + length] = plain[0, pl.ds(c, length, 2), :]
            else:
                strip = beside_v[num - 2].astype(F32)
                at = (pad - 1, pad + length)[num - 2]
                for c in range(2):
                    field[c, 1 : length + 1, at : at + 1] = strip[:, c : c + 1]

        @pl.when(jnp.logical_not(arrives))
        def _():
            for c in range(2):
                if num < 2:
                    field[c, (0, length + 1)[num], pad : pad + length] = jnp.zeros((length, LANES), F32)
                else:
                    at = (pad - 1, pad + length)[num - 2]
                    field[c, 1 : length + 1, at : at + 1] = jnp.zeros((length, 1, LANES), F32)

    locals_[1].wait()

    def residual_row(k, carry):
        slot = lax.rem(k, UNROLL)
        plain[slot] = source_v[k].astype(F32)
        wave_term = jnp.broadcast_to(
            pltpu.roll(coef_v[:length], lax.rem(LANES - k, LANES), 1)[:, :1], (length, LANES)
        )
        diagonal_term = 4.0 - wave_term
        damp = wave_term * DAMPING
        center = [field[c, k + 1, pad : pad + length] for c in range(2)]
        around = [
            field[c, k + 2, pad : pad + length]
            + field[c, k, pad : pad + length]
            + field[c, k + 1, pad + 1 : pad + 1 + length]
            + field[c, k + 1, pad - 1 : pad - 1 + length]
            for c in range(2)
        ]
        real_part = diagonal_term * center[0] + damp * center[1] - around[0]
        imag_part = diagonal_term * center[1] - damp * center[0] - around[1]
        real = (plain[slot, pl.ds(0, length, 2), :] - real_part).astype(BF16)
        imag = (plain[slot, pl.ds(1, length, 2), :] - imag_part).astype(BF16)
        at = pl.ds(pl.multiple_of(k * length, length), length)
        load_a[at, :LANES] = real
        load_a[at, LANES:] = imag
        load_b[at, :LANES] = -imag
        load_b[at, LANES:] = real
        return carry

    lax.fori_loop(0, length // 2, residual_row, 0, unroll=UNROLL)
    maps2[0].wait_recv()
    maps2[2].start()
    lax.fori_loop(length // 2, length, residual_row, 0, unroll=UNROLL)

    locals_[2].wait()
    leaf = dot1(body_v[0], load_a[...]) + dot1(body_v[1], load_b[...])
    inv_ref[...] = leaf
    for k in range(4):
        for c in range(2):
            h0[c, k * side : (k + 1) * side] = inv_ref[
                pl.ds(starts[k], side), c * LANES : (c + 1) * LANES
            ]
    first_h = remote(h0.at[:, :side], face1h, send1.at[1], recv1.at[1], (vertical, q))
    first_h.start()
    first_h.wait()
    wave = dot3(
        cross1[1],
        dot3(cross1[0], rows([h0[0, :side], h0[1, :side]])) - rows([face1h[0], face1h[1]]),
    )
    rest = m0[0, side:], m0[1, side:]
    gain = dot3(embed_low(tile(rest[0], 0), tile(rest[1], 0)), wave)
    for c in range(2):
        h1[c] = gain[c * count : (c + 1) * count] + h0[c, side:]
    data2 = exchange(h1.at[:, :side], face2h, 1)
    data2[0].start()
    data2[1].start()

    maps2[1].wait_recv()
    maps2[2].wait_recv()
    for copy in maps2:
        copy.wait_send()
    mine = rows([
        x for c in range(2) for x in (m1[c, :side], swapped_view(face2[0, c].astype(F32)))
    ])
    theirs = rows([
        x
        for c in range(2)
        for x in (face2[1, c].astype(F32), swapped_view(face2[2, c].astype(F32)))
    ])
    across = embed(theirs[: 2 * side, :LANES], theirs[2 * side :, :LANES])
    cross2[0] = across
    product = dot3(across, mine)
    turned = tile(product, 0)
    inv = inverse(embed(turned[: 2 * side], turned[2 * side :]), pow_ref, inv_ref)
    cross2[1] = inv
    wave = dot3(inv, cols([
        tile(product, 1), tile(product, 2), -tile(theirs, 1), -tile(theirs, 2),
    ]))
    rest = m1[0, side:], m1[1, side:]
    gain = dot3(embed(tile(rest[0], 0), tile(rest[1], 0)), wave)
    count2 = 2 * side
    for c in range(2):
        part = gain[c * count2 : (c + 1) * count2]
        t_own = tile(part, 0) + tile(rest[c], 1)
        t_vert = tile(part, 1) + tile(rest[c], 2)
        t_side = tile(part, 2)
        t_diag = tile(part, 3)
        own_0 = jnp.where(q_odd == 1, t_side, t_own)
        own_1 = jnp.where(q_odd == 1, t_own, t_side)
        vert_0 = jnp.where(q_odd == 1, t_diag, t_vert)
        vert_1 = jnp.where(q_odd == 1, t_vert, t_diag)
        in_0 = jnp.where(inner, own_0, vert_0)
        in_1 = jnp.where(inner, own_1, vert_1)
        out_0 = jnp.where(inner, vert_0, own_0)
        out_1 = jnp.where(inner, vert_1, own_1)
        m2[c, :, :LANES] = low_low(in_0, in_1)
        m2[c, :, LANES : 2 * LANES] = low_low(out_0, out_1)
        m2[c, :, 2 * LANES : 3 * LANES] = jnp.where(
            lower, high_high(out_1, in_1), high_high(in_1, out_1)
        )
        m2[c, :, 3 * LANES :] = jnp.where(
            lower, high_high(out_0, in_0), high_high(in_0, out_0)
        )
    out3[...] = m2[:, :side].astype(WIRE)

    def last_copies(src, face, kind):
        def send(source, box, slot, target):
            return remote(
                source, face.at[box, q_odd], send3.at[kind, slot], recv3.at[kind, slot], target
            )

        return (
            lambda: send(src, 0, 0, (vertical, q)),
            lambda: send(face.at[1, q_odd], 1, 1, (vertical, q)),
            lambda: send(src, 1, 2, (facing, q)),
            lambda: send(src, 0, 3, (p, beside)),
            lambda: send(face.at[0, q_odd], 0, 3, (p, beside)),
            lambda: send(face.at[1, q_odd], 1, 4, (p, beside)),
        )

    def last_start(copies, src, face):
        up_own, up_other, over, side_own, side_relay, side_other = copies

        @pl.when(inner)
        def _():
            over().start()
            up_own().start()
            side_own().start()
            face[0, q_odd] = src[:, :side]

    def last_relay(copies):
        up_own, up_other, over, side_own, side_relay, side_other = copies

        @pl.when(inner)
        def _():
            over().wait_recv()
            up_other().start()
            side_other().start()

        @pl.when(jnp.logical_not(inner))
        def _():
            up_own().wait_recv()
            side_relay().start()
            up_other().wait_recv()
            side_other().start()

    def last_wait(copies):
        up_own, up_other, over, side_own, side_relay, side_other = copies
        side_own().wait_recv()
        side_other().wait_recv()

    def last_drain(copies):
        up_own, up_other, over, side_own, side_relay, side_other = copies
        side_own().wait_send()
        side_other().wait_send()

        @pl.when(inner)
        def _():
            over().wait_send()
            up_own().wait_send()
            up_other().wait_send()

    maps3 = last_copies(out3, face3, 0)
    last_start(maps3, out3, face3)

    data2[0].wait_recv()
    data2[2].start()
    data2[1].wait_recv()
    data2[2].wait_recv()
    mine = rows([x for c in range(2) for x in (h1[c, :side], face2h[0, c])])
    theirs = rows([x for c in range(2) for x in (face2h[1, c], face2h[2, c])])
    wave = dot3(cross2[1], dot3(cross2[0], mine) - theirs)
    rest = m1[0, side:], m1[1, side:]
    gain = dot3(embed(tile(rest[0], 0), tile(rest[1], 0)), wave)
    for c in range(2):
        h2[c] = gain[c * count2 : (c + 1) * count2] + h1[c, side:]
    data3 = last_copies(h2.at[:, :side], face3h, 1)
    last_start(data3, h2, face3h)
    last_relay(maps3)
    last_relay(data3)

    last_wait(maps3)
    mine = rows([face3[0, j, c].astype(F32) for c in range(2) for j in range(2)])
    theirs = rows([face3[1, j, c].astype(F32) for c in range(2) for j in range(2)])
    across = embed(theirs[: 2 * side, :LANES], theirs[2 * side :, :LANES])
    product = dot3(across, mine)
    turned = tile(product, 0)
    inv = inverse(embed(turned[: 2 * side], turned[2 * side :]), pow_ref, inv_ref)
    begin = pl.multiple_of(inner_num * side, side)
    rest = m2[0, pl.ds(begin, side)], m2[1, pl.ds(begin, side)]
    out_gain = dot3(embed(tile(rest[0], 0), tile(rest[1], 0)), inv)
    cross3[0] = across
    cross3[1, : 2 * side] = out_gain
    gain = dot3(out_gain, cols(
        [tile(product, k) for k in range(1, 4)] + [-tile(theirs, k) for k in range(1, 4)]
    ))
    for c in range(2):
        part = gain[c * side : (c + 1) * side]
        own = [tile(part, k) + tile(rest[c], k + 1) for k in range(3)]
        other = [tile(part, k + 3) for k in range(3)]
        low = [jnp.where(lower, a, b) for a, b in zip(own, other)]
        up = [jnp.where(lower, b, a) for a, b in zip(own, other)]
        for k, value in enumerate([low[0], low[1], low[2], up[1], up[0], up[2]]):
            top_ref[c, :, k * LANES : (k + 1) * LANES] = value
    last_wait(data3)
    mine = rows([face3h[0, j, c] for c in range(2) for j in range(2)])
    theirs = rows([face3h[1, j, c] for c in range(2) for j in range(2)])
    gain = dot3(cross3[1, : 2 * side], dot3(cross3[0], mine) - theirs)
    for c in range(2):
        top_out_ref[c] = gain[c * side : (c + 1) * side] + h2[c, pl.ds(begin, side)]
    for copy in data2:
        copy.wait_send()
    last_drain(maps3)
    last_drain(data3)
    for exists, _, _, copy in halos:

        @pl.when(exists)
        def _():
            copy().wait_send()


def place_kernel(map_ref, out_ref, top_ref, top_out_ref):
    top_ref[...] = map_ref[...]
    top_out_ref[...] = out_ref[...]


def on_device(source, guess, coefficient, leaf_map, body_map):
    length, width, _, rhs = guess.shape
    order = leaf_map.shape[3]
    side = order // 4
    vmem = pl.BlockSpec(memory_space=pltpu.VMEM)
    hbm = pl.BlockSpec(memory_space=pl.ANY)
    dma = pltpu.SemaphoreType.DMA
    rows_of = lambda x: x.reshape(length, 2 * width, rhs)
    own_map, own_out = pl.pallas_call(
        tree_kernel,
        name="build_tree",
        out_shape=(
            jax.ShapeDtypeStruct((2, side, 12 * side), F32),
            jax.ShapeDtypeStruct((2, side, rhs), F32),
        ),
        in_specs=[hbm, hbm, hbm, vmem, vmem, hbm],
        out_specs=(vmem, vmem),
        scratch_shapes=[
            pltpu.VMEM((length, 2 * width, rhs), BF16),
            pltpu.VMEM((length, 2 * width, rhs), BF16),
            pltpu.VMEM((2, order, length * width), BF16),
            pltpu.VMEM((2, 2 * width, rhs), BF16),
            pltpu.VMEM((2, length, 2, rhs), BF16),
            pltpu.VMEM((LANES, LANES), F32),
            pltpu.VMEM((UNROLL, 2 * width, rhs), F32),
            pltpu.VMEM((2, length + 2, width + 16, rhs), F32),
            pltpu.VMEM((length * width, 2 * rhs), BF16),
            pltpu.VMEM((length * width, 2 * rhs), BF16),
            pltpu.VMEM((2, order, order), F32),
            pltpu.VMEM((2, order, rhs), F32),
            pltpu.VMEM((2, 3 * side, 6 * side), F32),
            pltpu.VMEM((2, 3 * side, rhs), F32),
            pltpu.VMEM((2, 2 * side, 8 * side), F32),
            pltpu.VMEM((2, 2 * side, rhs), F32),
            pltpu.VMEM((2, side, 6 * side), WIRE),
            pltpu.VMEM((2, side, 8 * side), WIRE),
            pltpu.VMEM((2, side, order), F32),
            pltpu.VMEM((2, side, rhs), F32),
            pltpu.VMEM((3, 2, side, 6 * side), WIRE),
            pltpu.VMEM((3, 2, side, rhs), F32),
            pltpu.VMEM((2, 2, 2, side, 8 * side), WIRE),
            pltpu.VMEM((2, 2, 2, side, rhs), F32),
            pltpu.VMEM((order, order), F32),
            pltpu.VMEM((order, order), F32),
            pltpu.VMEM((2, 2 * side, 2 * side), F32),
            pltpu.VMEM((2, order, order), F32),
            pltpu.VMEM((2, order, order), F32),
            dma((3,)), dma((4,)), dma((4,)), dma((2,)), dma((2,)),
            dma((2, 3)), dma((2, 3)), dma((2, 5)), dma((2, 5)),
        ],
        compiler_params=pltpu.CompilerParams(
            collective_id=0, has_side_effects=True, vmem_limit_bytes=56 * 1024 * 1024
        ),
    )(guess, rows_of(guess), rows_of(source), coefficient, leaf_map[0, 0], body_map[0, 0])
    own_map, own_out = pl.pallas_call(
        place_kernel,
        name="place",
        out_shape=(
            jax.ShapeDtypeStruct(own_map.shape, F32),
            jax.ShapeDtypeStruct(own_out.shape, F32),
        ),
        in_specs=[vmem, vmem],
        out_specs=(vmem, vmem),
    )(own_map, own_out)
    return (own_map[None, None], own_out[None, None])


def solution(mesh):
    placed = (
        P("tx", "ty", None, None),
        P("tx", "ty", None, None),
        P("tx", "ty"),
        P("tx", "ty", None, None, None),
        P("tx", "ty", None, None, None),
    )
    return jax.shard_map(
        on_device,
        mesh=mesh,
        in_specs=placed,
        out_specs=(P("tx", "ty", None, None, None), P("tx", "ty", None, None, None)),
        check_vma=False,
    )
```

```python
import functools

import jax
import jax.numpy as jnp
from jax import lax
from jax.experimental import pallas as pl
from jax.experimental.pallas import tpu as pltpu
from jax.sharding import PartitionSpec as P

DAMPING = 0.5
DOUBLINGS = 7
FINE = 2
LANES = 128
MESH = pl.DeviceIdType.MESH
F32 = jnp.float32
BF16 = jnp.bfloat16
WIRE = BF16
UNROLL = 4


def split(x):
    high = x.astype(BF16)
    return high, (x - high.astype(F32)).astype(BF16)


def dot1(a, b):
    return jnp.dot(a, b, preferred_element_type=F32)


def dot3(a, b):
    a_high, a_low = split(a)
    b_high, b_low = split(b)
    return dot1(a_high, b_high) + (dot1(a_high, b_low) + dot1(a_low, b_high))


def tile(x, k):
    return x[:, k * LANES : (k + 1) * LANES]


def cols(parts):
    return jnp.concatenate(parts, axis=1)


def rows(parts):
    return jnp.concatenate(parts, axis=0)


def half_roll(x):
    return pltpu.roll(x, LANES // 2, 1)


def low_lanes(shape):
    return lax.broadcasted_iota(jnp.int32, shape, 1) < LANES // 2


def low_low(a, b):
    return jnp.where(low_lanes(a.shape), a, half_roll(b))


def high_high(a, b):
    return jnp.where(low_lanes(a.shape), half_roll(a), b)


def embed(re, im):
    return rows([cols([re, -im]), cols([im, re])])


def embed_low(re, im):
    return rows([low_low(re, -im), low_low(im, re)])


def identity(n):
    return (
        lax.broadcasted_iota(jnp.int32, (n, n), 0) == lax.broadcasted_iota(jnp.int32, (n, n), 1)
    ).astype(F32)


def inverse(power, pow_ref, inv_ref):
    n = power.shape[0]
    total = identity(n) + power
    now = dot3(power, power)
    for _ in range(FINE):
        both = dot3(now, cols([now, total]))
        now, total = both[:, :n], total + both[:, n:]
    pow_ref[:n, :n] = now.astype(BF16)
    inv_ref[:n, :n] = total

    def body(k, carry):
        now, total = pow_ref[:n, :n], inv_ref[:n, :n]
        both = dot1(now, cols([now, total.astype(BF16)]))
        pow_ref[:n, :n] = both[:, :n].astype(BF16)
        inv_ref[:n, :n] = total + both[:, n:]
        return carry

    lax.fori_loop(0, DOUBLINGS - 2 - FINE, body, 0)
    total = inv_ref[:n, :n]
    return total + dot1(pow_ref[:n, :n], total.astype(BF16))


def swapped_view(block):
    return cols([half_roll(tile(block, 0)), tile(block, 2), tile(block, 1)])


def tree_kernel(
    guess_ref, guess_rows_ref, source_ref, coef_hbm, map_hbm, body_ref, top_ref, top_out_ref,
    guess_v, source_v, body_v, coef_ref, map_ref, edge_v, beside_v, coef_v, plain, field, load_a, load_b,
    m0, h0, m1, h1, m2, h2, out1, out2, out3,
    face1, face1h, face2, face2h, face3, face3h, pow_ref, inv_ref, cross1, cross2, cross3,
    local_sem, halo_send, halo_recv, send1, recv1, send2, recv2, send3, recv3,
):
    p = lax.axis_index("tx")
    q = lax.axis_index("ty")
    p_ends = lax.axis_size("tx") - 1
    q_ends = lax.axis_size("ty") - 1
    p_low = lax.rem(p, 4)
    p_odd = lax.rem(p, 2)
    q_odd = lax.rem(q, 2)
    vertical = p + 1 - 2 * p_odd
    beside = q + 1 - 2 * q_odd
    inner = (p_low == 1) | (p_low == 2)
    inner_num = jnp.where(inner, 1, 0)
    lower = p_low < 2
    facing = p + 3 - 2 * p_low
    side = map_ref.shape[1] // 4
    length = guess_ref.shape[0]
    last = length - 1

    def remote(src, dst, send, recv, target):
        return pltpu.make_async_remote_copy(
            src_ref=src, dst_ref=dst, send_sem=send, recv_sem=recv,
            device_id=target, device_id_type=MESH,
        )

    halos = [
        (p < p_ends, p > 0, (p + 1, q),
         lambda: remote(guess_rows_ref.at[last], edge_v.at[0], halo_send.at[0], halo_recv.at[0], (p + 1, q))),
        (p > 0, p < p_ends, (p - 1, q),
         lambda: remote(guess_rows_ref.at[0], edge_v.at[1], halo_send.at[1], halo_recv.at[1], (p - 1, q))),
        (q < q_ends, q > 0, (p, q + 1),
         lambda: remote(guess_ref.at[:, last], beside_v.at[0], halo_send.at[2], halo_recv.at[2], (p, q + 1))),
        (q > 0, q < q_ends, (p, q - 1),
         lambda: remote(guess_ref.at[:, 0], beside_v.at[1], halo_send.at[3], halo_recv.at[3], (p, q - 1))),
    ]
    early = [
        pltpu.make_async_copy(map_hbm, map_ref, local_sem.at[3]),
        pltpu.make_async_copy(coef_hbm, coef_ref, local_sem.at[4]),
    ]
    for copy in early:
        copy.start()
    locals_ = [
        pltpu.make_async_copy(guess_rows_ref, guess_v, local_sem.at[0]),
        pltpu.make_async_copy(source_ref, source_v, local_sem.at[1]),
        pltpu.make_async_copy(body_ref, body_v, local_sem.at[2]),
    ]
    for copy in locals_:
        copy.start()
    barrier = pltpu.get_barrier_semaphore()
    arrivals = 0
    for exists, _, target, _ in halos:
        arrivals = arrivals + jnp.where(exists, 1, 0)

        @pl.when(exists)
        def _():
            pl.semaphore_signal(barrier, inc=1, device_id=target, device_id_type=MESH)

    pl.semaphore_wait(barrier, arrivals)
    for exists, _, _, copy in halos:

        @pl.when(exists)
        def _():
            copy().start()

    starts = [
        jnp.where(p_odd == 1, 0, 2 * side),
        jnp.where(q_odd == 1, 3 * side, side),
        jnp.where(p_odd == 1, 2 * side, 0),
        jnp.where(q_odd == 1, side, 3 * side),
    ]
    starts = [pl.multiple_of(begin, side) for begin in starts]
    lane = lax.broadcasted_iota(jnp.int32, (side, LANES), 1)
    vert_swap = jnp.where(p_odd == 1, 0, 1)
    cross = jnp.where(lane < LANES // 2, vert_swap, q_odd) == 1

    for copy in early:
        copy.wait()
    first = remote(out1, face1, send1.at[0], recv1.at[0], (vertical, q))
    for k in range(4):
        for c in range(2):
            left = map_ref[c, pl.ds(starts[k], side), :LANES]
            right = map_ref[c, pl.ds(starts[k], side), LANES:]
            m0[c, k * side : (k + 1) * side, :LANES] = jnp.where(cross, right, left)
            m0[c, k * side : (k + 1) * side, LANES:] = jnp.where(cross, left, right)
        if k == 0:
            out1[...] = m0[:, :side].astype(WIRE)
            first.start()

    pad = 8
    locals_[0].wait()

    def apart(k, carry):
        slot = lax.rem(k, UNROLL)
        plain[slot] = guess_v[k].astype(F32)
        for c in range(2):
            field[c, k + 1, pad : pad + length] = plain[slot, pl.ds(c, length, 2), :]
        return carry

    lax.fori_loop(0, length, apart, 0, unroll=UNROLL)
    coef_v[...] = jnp.zeros_like(coef_v)
    coef_v[:length, :length] = coef_ref[...]
    coef_t = jnp.transpose(coef_v[...])[:length]
    coef_v[:length] = coef_t
    first.wait()
    mine = rows([m0[0, :side], m0[1, :side]])
    theirs = rows([face1[0].astype(F32), face1[1].astype(F32)])
    across = embed_low(theirs[:side, :LANES], theirs[side:, :LANES])
    cross1[0] = across
    product = dot3(across, mine)
    turned = tile(product, 0)
    inv = inverse(embed_low(turned[:side], turned[side:]), pow_ref, inv_ref)
    cross1[1] = inv
    wave = dot3(inv, cols([
        jnp.where(low_lanes(turned.shape), half_roll(turned), -tile(theirs, 0)),
        tile(product, 1),
        -tile(theirs, 1),
    ]))
    rest = m0[0, side:], m0[1, side:]
    gain = dot3(embed_low(tile(rest[0], 0), tile(rest[1], 0)), wave)
    count = 3 * side
    for c in range(2):
        part = gain[c * count : (c + 1) * count]
        first_tile = tile(rest[c], 0)
        m1[c, :, :LANES] = tile(part, 0) + jnp.where(
            low_lanes(first_tile.shape), half_roll(first_tile), 0.0
        )
        m1[c, :, LANES : 2 * LANES] = tile(part, 1) + tile(rest[c], 1)
        m1[c, :, 2 * LANES :] = tile(part, 2)
    out2[...] = m1[:, :side].astype(WIRE)

    def exchange(src, face, kind):
        return (
            remote(src, face.at[0], send2.at[kind, 0], recv2.at[kind, 0], (vertical, q)),
            remote(src, face.at[1], send2.at[kind, 1], recv2.at[kind, 1], (p, beside)),
            remote(face.at[0], face.at[2], send2.at[kind, 2], recv2.at[kind, 2], (p, beside)),
        )

    maps2 = exchange(out2, face2, 0)
    maps2[0].start()
    maps2[1].start()

    for num, (exists, arrives, _, copy) in enumerate(halos):

        @pl.when(arrives)
        def _():
            copy().wait_recv()
            if num < 2:
                plain[0] = edge_v[num].astype(F32)
                for c in range(2):
                    field[c, (0, length + 1)[num], pad : pad + length] = plain[0, pl.ds(c, length, 2), :]
            else:
                strip = beside_v[num - 2].astype(F32)
                at = (pad - 1, pad + length)[num - 2]
                for c in range(2):
                    field[c, 1 : length + 1, at : at + 1] = strip[:, c : c + 1]

        @pl.when(jnp.logical_not(arrives))
        def _():
            for c in range(2):
                if num < 2:
                    field[c, (0, length + 1)[num], pad : pad + length] = jnp.zeros((length, LANES), F32)
                else:
                    at = (pad - 1, pad + length)[num - 2]
                    field[c, 1 : length + 1, at : at + 1] = jnp.zeros((length, 1, LANES), F32)

    locals_[1].wait()

    def residual_row(k, carry):
        slot = lax.rem(k, UNROLL)
        plain[slot] = source_v[k].astype(F32)
        wave_term = jnp.broadcast_to(
            pltpu.roll(coef_v[:length], lax.rem(LANES - k, LANES), 1)[:, :1], (length, LANES)
        )
        diagonal_term = 4.0 - wave_term
        damp = wave_term * DAMPING
        center = [field[c, k + 1, pad : pad + length] for c in range(2)]
        around = [
            field[c, k + 2, pad : pad + length]
            + field[c, k, pad : pad + length]
            + field[c, k + 1, pad + 1 : pad + 1 + length]
            + field[c, k + 1, pad - 1 : pad - 1 + length]
            for c in range(2)
        ]
        real_part = diagonal_term * center[0] + damp * center[1] - around[0]
        imag_part = diagonal_term * center[1] - damp * center[0] - around[1]
        real = (plain[slot, pl.ds(0, length, 2), :] - real_part).astype(BF16)
        imag = (plain[slot, pl.ds(1, length, 2), :] - imag_part).astype(BF16)
        at = pl.ds(pl.multiple_of(k * length, length), length)
        load_a[at, :LANES] = real
        load_a[at, LANES:] = imag
        load_b[at, :LANES] = -imag
        load_b[at, LANES:] = real
        return carry

    lax.fori_loop(0, length // 2, residual_row, 0, unroll=UNROLL)
    maps2[0].wait_recv()
    maps2[2].start()
    lax.fori_loop(length // 2, length, residual_row, 0, unroll=UNROLL)

    locals_[2].wait()
    leaf = dot1(body_v[0], load_a[...]) + dot1(body_v[1], load_b[...])
    inv_ref[...] = leaf
    for k in range(4):
        for c in range(2):
            h0[c, k * side : (k + 1) * side] = inv_ref[
                pl.ds(starts[k], side), c * LANES : (c + 1) * LANES
            ]
    first_h = remote(h0.at[:, :side], face1h, send1.at[1], recv1.at[1], (vertical, q))
    first_h.start()
    first_h.wait()
    wave = dot3(
        cross1[1],
        dot3(cross1[0], rows([h0[0, :side], h0[1, :side]])) - rows([face1h[0], face1h[1]]),
    )
    rest = m0[0, side:], m0[1, side:]
    gain = dot3(embed_low(tile(rest[0], 0), tile(rest[1], 0)), wave)
    for c in range(2):
        h1[c] = gain[c * count : (c + 1) * count] + h0[c, side:]
    data2 = exchange(h1.at[:, :side], face2h, 1)
    data2[0].start()
    data2[1].start()

    maps2[1].wait_recv()
    maps2[2].wait_recv()
    for copy in maps2:
        copy.wait_send()
    mine = rows([
        x for c in range(2) for x in (m1[c, :side], swapped_view(face2[0, c].astype(F32)))
    ])
    theirs = rows([
        x
        for c in range(2)
        for x in (face2[1, c].astype(F32), swapped_view(face2[2, c].astype(F32)))
    ])
    across = embed(theirs[: 2 * side, :LANES], theirs[2 * side :, :LANES])
    cross2[0] = across
    product = dot3(across, mine)
    turned = tile(product, 0)
    inv = inverse(embed(turned[: 2 * side], turned[2 * side :]), pow_ref, inv_ref)
    cross2[1] = inv
    wave = dot3(inv, cols([
        tile(product, 1), tile(product, 2), -tile(theirs, 1), -tile(theirs, 2),
    ]))
    rest = m1[0, side:], m1[1, side:]
    gain = dot3(embed(tile(rest[0], 0), tile(rest[1], 0)), wave)
    count2 = 2 * side
    for c in range(2):
        part = gain[c * count2 : (c + 1) * count2]
        t_own = tile(part, 0) + tile(rest[c], 1)
        t_vert = tile(part, 1) + tile(rest[c], 2)
        t_side = tile(part, 2)
        t_diag = tile(part, 3)
        own_0 = jnp.where(q_odd == 1, t_side, t_own)
        own_1 = jnp.where(q_odd == 1, t_own, t_side)
        vert_0 = jnp.where(q_odd == 1, t_diag, t_vert)
        vert_1 = jnp.where(q_odd == 1, t_vert, t_diag)
        in_0 = jnp.where(inner, own_0, vert_0)
        in_1 = jnp.where(inner, own_1, vert_1)
        out_0 = jnp.where(inner, vert_0, own_0)
        out_1 = jnp.where(inner, vert_1, own_1)
        m2[c, :, :LANES] = low_low(in_0, in_1)
        m2[c, :, LANES : 2 * LANES] = low_low(out_0, out_1)
        m2[c, :, 2 * LANES : 3 * LANES] = jnp.where(
            lower, high_high(out_1, in_1), high_high(in_1, out_1)
        )
        m2[c, :, 3 * LANES :] = jnp.where(
            lower, high_high(out_0, in_0), high_high(in_0, out_0)
        )
    out3[...] = m2[:, :side].astype(WIRE)

    def last_copies(src, face, kind):
        first_rows = src
        def send(source, box, slot, target):
            return remote(
                source, face.at[box, q_odd], send3.at[kind, slot], recv3.at[kind, slot], target
            )

        def plane(source, slot, target):
            return [
                lambda c=c: remote(
                    source(c), face.at[1, q_odd, c],
                    send3.at[kind, slot + c], recv3.at[kind, slot + c], target,
                )
                for c in range(2)
            ]

        return (
            lambda: send(src, 0, 0, (vertical, q)),
            plane(lambda c: face.at[1, q_odd, c], 2, (vertical, q)),
            plane(lambda c: first_rows.at[c], 4, (facing, q)),
            lambda: send(src, 0, 1, (p, beside)),
            lambda: send(face.at[0, q_odd], 0, 1, (p, beside)),
            plane(lambda c: face.at[1, q_odd, c], 6, (p, beside)),
        )

    def last_start(copies, src, face):
        up_own, up_other, over, side_own, side_relay, side_other = copies

        @pl.when(inner)
        def _():
            for c in range(2):
                over[c]().start()
            up_own().start()
            side_own().start()
            face[0, q_odd] = src[:, :side]

    def inner_relay(copies):
        up_own, up_other, over, side_own, side_relay, side_other = copies

        @pl.when(inner)
        def _():
            for c in range(2):
                over[c]().wait_recv()
                up_other[c]().start()
                side_other[c]().start()

    def outer_relay(copies):
        up_own, up_other, over, side_own, side_relay, side_other = copies

        @pl.when(jnp.logical_not(inner))
        def _():
            up_own().wait_recv()
            side_relay().start()
            for c in range(2):
                up_other[c]().wait_recv()
                side_other[c]().start()

    def last_wait(copies):
        up_own, up_other, over, side_own, side_relay, side_other = copies
        side_own().wait_recv()
        for c in range(2):
            side_other[c]().wait_recv()

    def last_drain(copies):
        up_own, up_other, over, side_own, side_relay, side_other = copies
        side_own().wait_send()
        for c in range(2):
            side_other[c]().wait_send()

        @pl.when(inner)
        def _():
            up_own().wait_send()
            for c in range(2):
                over[c]().wait_send()
                up_other[c]().wait_send()

    maps3 = last_copies(out3, face3, 0)
    last_start(maps3, out3, face3)

    data2[0].wait_recv()
    data2[2].start()
    data2[1].wait_recv()
    data2[2].wait_recv()
    mine = rows([x for c in range(2) for x in (h1[c, :side], face2h[0, c])])
    theirs = rows([x for c in range(2) for x in (face2h[1, c], face2h[2, c])])
    wave = dot3(cross2[1], dot3(cross2[0], mine) - theirs)
    rest = m1[0, side:], m1[1, side:]
    gain = dot3(embed(tile(rest[0], 0), tile(rest[1], 0)), wave)
    for c in range(2):
        h2[c] = gain[c * count2 : (c + 1) * count2] + h1[c, side:]
    data3 = last_copies(h2.at[:, :side], face3h, 1)
    last_start(data3, h2, face3h)
    inner_relay(maps3)
    outer_relay(maps3)
    inner_relay(data3)

    last_wait(maps3)
    mine = rows([face3[0, j, c].astype(F32) for c in range(2) for j in range(2)])
    theirs = rows([face3[1, j, c].astype(F32) for c in range(2) for j in range(2)])
    across = embed(theirs[: 2 * side, :LANES], theirs[2 * side :, :LANES])
    product = dot3(across, mine)
    turned = tile(product, 0)
    inv = inverse(embed(turned[: 2 * side], turned[2 * side :]), pow_ref, inv_ref)
    begin = pl.multiple_of(inner_num * side, side)
    rest = m2[0, pl.ds(begin, side)], m2[1, pl.ds(begin, side)]
    out_gain = dot3(embed(tile(rest[0], 0), tile(rest[1], 0)), inv)
    cross3[0] = across
    cross3[1, : 2 * side] = out_gain
    gain = dot3(out_gain, cols(
        [tile(product, k) for k in range(1, 4)] + [-tile(theirs, k) for k in range(1, 4)]
    ))
    for c in range(2):
        part = gain[c * side : (c + 1) * side]
        own = [tile(part, k) + tile(rest[c], k + 1) for k in range(3)]
        other = [tile(part, k + 3) for k in range(3)]
        low = [jnp.where(lower, a, b) for a, b in zip(own, other)]
        up = [jnp.where(lower, b, a) for a, b in zip(own, other)]
        for k, value in enumerate([low[0], low[1], low[2], up[1], up[0], up[2]]):
            top_ref[c, :, k * LANES : (k + 1) * LANES] = value
    outer_relay(data3)
    last_wait(data3)
    mine = rows([face3h[0, j, c] for c in range(2) for j in range(2)])
    theirs = rows([face3h[1, j, c] for c in range(2) for j in range(2)])
    gain = dot3(cross3[1, : 2 * side], dot3(cross3[0], mine) - theirs)
    for c in range(2):
        top_out_ref[c] = gain[c * side : (c + 1) * side] + h2[c, pl.ds(begin, side)]
    for copy in data2:
        copy.wait_send()
    last_drain(maps3)
    last_drain(data3)
    for exists, _, _, copy in halos:

        @pl.when(exists)
        def _():
            copy().wait_send()


def place_kernel(map_ref, out_ref, top_ref, top_out_ref):
    top_ref[...] = map_ref[...]
    top_out_ref[...] = out_ref[...]


def on_device(source, guess, coefficient, leaf_map, body_map):
    length, width, _, rhs = guess.shape
    order = leaf_map.shape[3]
    side = order // 4
    vmem = pl.BlockSpec(memory_space=pltpu.VMEM)
    hbm = pl.BlockSpec(memory_space=pl.ANY)
    dma = pltpu.SemaphoreType.DMA
    rows_of = lambda x: x.reshape(length, 2 * width, rhs)
    own_map, own_out = pl.pallas_call(
        tree_kernel,
        name="build_tree",
        out_shape=(
            jax.ShapeDtypeStruct((2, side, 12 * side), F32),
            jax.ShapeDtypeStruct((2, side, rhs), F32),
        ),
        in_specs=[hbm] * 6,
        out_specs=(vmem, vmem),
        scratch_shapes=[
            pltpu.VMEM((length, 2 * width, rhs), BF16),
            pltpu.VMEM((length, 2 * width, rhs), BF16),
            pltpu.VMEM((2, order, length * width), BF16),
            pltpu.VMEM((length, width), F32),
            pltpu.VMEM((2, order, order), F32),
            pltpu.VMEM((2, 2 * width, rhs), BF16),
            pltpu.VMEM((2, length, 2, rhs), BF16),
            pltpu.VMEM((LANES, LANES), F32),
            pltpu.VMEM((UNROLL, 2 * width, rhs), F32),
            pltpu.VMEM((2, length + 2, width + 16, rhs), F32),
            pltpu.VMEM((length * width, 2 * rhs), BF16),
            pltpu.VMEM((length * width, 2 * rhs), BF16),
            pltpu.VMEM((2, order, order), F32),
            pltpu.VMEM((2, order, rhs), F32),
            pltpu.VMEM((2, 3 * side, 6 * side), F32),
            pltpu.VMEM((2, 3 * side, rhs), F32),
            pltpu.VMEM((2, 2 * side, 8 * side), F32),
            pltpu.VMEM((2, 2 * side, rhs), F32),
            pltpu.VMEM((2, side, order), WIRE),
            pltpu.VMEM((2, side, 6 * side), WIRE),
            pltpu.VMEM((2, side, 8 * side), WIRE),
            pltpu.VMEM((2, side, order), WIRE),
            pltpu.VMEM((2, side, rhs), F32),
            pltpu.VMEM((3, 2, side, 6 * side), WIRE),
            pltpu.VMEM((3, 2, side, rhs), F32),
            pltpu.VMEM((2, 2, 2, side, 8 * side), WIRE),
            pltpu.VMEM((2, 2, 2, side, rhs), F32),
            pltpu.VMEM((order, order), BF16),
            pltpu.VMEM((order, order), F32),
            pltpu.VMEM((2, 2 * side, 2 * side), F32),
            pltpu.VMEM((2, order, order), F32),
            pltpu.VMEM((2, order, order), F32),
            dma((5,)), dma((4,)), dma((4,)), dma((2,)), dma((2,)),
            dma((2, 3)), dma((2, 3)), dma((2, 8)), dma((2, 8)),
        ],
        compiler_params=pltpu.CompilerParams(
            collective_id=0, has_side_effects=True, vmem_limit_bytes=56 * 1024 * 1024
        ),
    )(guess, rows_of(guess), rows_of(source), coefficient, leaf_map[0, 0], body_map[0, 0])
    own_map, own_out = pl.pallas_call(
        place_kernel,
        name="place",
        out_shape=(
            jax.ShapeDtypeStruct(own_map.shape, F32),
            jax.ShapeDtypeStruct(own_out.shape, F32),
        ),
        in_specs=[vmem, vmem],
        out_specs=(vmem, vmem),
    )(own_map, own_out)
    return (own_map[None, None], own_out[None, None])


def solution(mesh):
    placed = (
        P("tx", "ty", None, None),
        P("tx", "ty", None, None),
        P("tx", "ty"),
        P("tx", "ty", None, None, None),
        P("tx", "ty", None, None, None),
    )
    return jax.shard_map(
        on_device,
        mesh=mesh,
        in_specs=placed,
        out_specs=(P("tx", "ty", None, None, None), P("tx", "ty", None, None, None)),
        check_vma=False,
    )
```

```python
import functools

import jax
import jax.numpy as jnp
from jax import lax
from jax.experimental import pallas as pl
from jax.experimental.pallas import tpu as pltpu
from jax.sharding import PartitionSpec as P

DAMPING = 0.5
DOUBLINGS = 7
FINE = 2
LANES = 128
MESH = pl.DeviceIdType.MESH
F32 = jnp.float32
BF16 = jnp.bfloat16
WIRE = BF16
UNROLL = 4


def split(x):
    high = x.astype(BF16)
    return high, (x - high.astype(F32)).astype(BF16)


def dot1(a, b):
    return jnp.dot(a, b, preferred_element_type=F32)


def dot3(a, b):
    a_high, a_low = split(a)
    b_high, b_low = split(b)
    return dot1(a_high, b_high) + (dot1(a_high, b_low) + dot1(a_low, b_high))


def dotw(a, b):
    return dot1(a.astype(BF16), b.astype(BF16))


def tile(x, k):
    return x[:, k * LANES : (k + 1) * LANES]


def cols(parts):
    return jnp.concatenate(parts, axis=1)


def rows(parts):
    return jnp.concatenate(parts, axis=0)


def half_roll(x):
    return pltpu.roll(x, LANES // 2, 1)


def low_lanes(shape):
    return lax.broadcasted_iota(jnp.int32, shape, 1) < LANES // 2


def low_low(a, b):
    return jnp.where(low_lanes(a.shape), a, half_roll(b))


def high_high(a, b):
    return jnp.where(low_lanes(a.shape), half_roll(a), b)


def embed(re, im):
    return rows([cols([re, -im]), cols([im, re])])


def embed_low(re, im):
    return rows([low_low(re, -im), low_low(im, re)])


def identity(n):
    return (
        lax.broadcasted_iota(jnp.int32, (n, n), 0) == lax.broadcasted_iota(jnp.int32, (n, n), 1)
    ).astype(F32)


def inverse(power, pow_ref, inv_ref):
    n = power.shape[0]
    total = identity(n) + power
    now = dot3(power, power)
    for _ in range(FINE):
        both = dot3(now, cols([now, total]))
        now, total = both[:, :n], total + both[:, n:]
    pow_ref[:n, :n] = now.astype(BF16)
    inv_ref[:n, :n] = total

    def body(k, carry):
        now, total = pow_ref[:n, :n], inv_ref[:n, :n]
        both = dot1(now, cols([now, total.astype(BF16)]))
        pow_ref[:n, :n] = both[:, :n].astype(BF16)
        inv_ref[:n, :n] = total + both[:, n:]
        return carry

    lax.fori_loop(0, DOUBLINGS - 2 - FINE, body, 0)
    total = inv_ref[:n, :n]
    return total + dot1(pow_ref[:n, :n], total.astype(BF16))


def swapped_view(block):
    return cols([half_roll(tile(block, 0)), tile(block, 2), tile(block, 1)])


def tree_kernel(
    guess_ref, guess_rows_ref, source_ref, coef_hbm, map_hbm, body_ref, top_ref, top_out_ref,
    guess_v, source_v, body_v, coef_ref, map_ref, edge_v, beside_v, coef_v, plain, field, load_a, load_b,
    m0, h0, m1, h1, m2, h2, out1, out2, out3,
    face1, face1h, face2, face2h, face3, face3h, pow_ref, inv_ref, cross1, cross2, cross3,
    local_sem, halo_send, halo_recv, send1, recv1, send2, recv2, send3, recv3,
):
    p = lax.axis_index("tx")
    q = lax.axis_index("ty")
    p_ends = lax.axis_size("tx") - 1
    q_ends = lax.axis_size("ty") - 1
    p_low = lax.rem(p, 4)
    p_odd = lax.rem(p, 2)
    q_odd = lax.rem(q, 2)
    vertical = p + 1 - 2 * p_odd
    beside = q + 1 - 2 * q_odd
    inner = (p_low == 1) | (p_low == 2)
    inner_num = jnp.where(inner, 1, 0)
    lower = p_low < 2
    facing = p + 3 - 2 * p_low
    side = map_ref.shape[1] // 4
    length = guess_ref.shape[0]
    last = length - 1

    def remote(src, dst, send, recv, target):
        return pltpu.make_async_remote_copy(
            src_ref=src, dst_ref=dst, send_sem=send, recv_sem=recv,
            device_id=target, device_id_type=MESH,
        )

    halos = [
        (p < p_ends, p > 0, (p + 1, q),
         lambda: remote(guess_rows_ref.at[last], edge_v.at[0], halo_send.at[0], halo_recv.at[0], (p + 1, q))),
        (p > 0, p < p_ends, (p - 1, q),
         lambda: remote(guess_rows_ref.at[0], edge_v.at[1], halo_send.at[1], halo_recv.at[1], (p - 1, q))),
        (q < q_ends, q > 0, (p, q + 1),
         lambda: remote(guess_ref.at[:, last], beside_v.at[0], halo_send.at[2], halo_recv.at[2], (p, q + 1))),
        (q > 0, q < q_ends, (p, q - 1),
         lambda: remote(guess_ref.at[:, 0], beside_v.at[1], halo_send.at[3], halo_recv.at[3], (p, q - 1))),
    ]
    early = [
        pltpu.make_async_copy(map_hbm, map_ref, local_sem.at[3]),
        pltpu.make_async_copy(coef_hbm, coef_ref, local_sem.at[4]),
    ]
    for copy in early:
        copy.start()
    locals_ = [
        pltpu.make_async_copy(guess_rows_ref, guess_v, local_sem.at[0]),
        pltpu.make_async_copy(source_ref, source_v, local_sem.at[1]),
        pltpu.make_async_copy(body_ref, body_v, local_sem.at[2]),
    ]
    for copy in locals_:
        copy.start()
    barrier = pltpu.get_barrier_semaphore()
    arrivals = 0
    for exists, _, target, _ in halos:
        arrivals = arrivals + jnp.where(exists, 1, 0)

        @pl.when(exists)
        def _():
            pl.semaphore_signal(barrier, inc=1, device_id=target, device_id_type=MESH)

    pl.semaphore_wait(barrier, arrivals)
    starts = [
        jnp.where(p_odd == 1, 0, 2 * side),
        jnp.where(q_odd == 1, 3 * side, side),
        jnp.where(p_odd == 1, 2 * side, 0),
        jnp.where(q_odd == 1, side, 3 * side),
    ]
    starts = [pl.multiple_of(begin, side) for begin in starts]
    lane = lax.broadcasted_iota(jnp.int32, (side, LANES), 1)
    vert_swap = jnp.where(p_odd == 1, 0, 1)
    cross = jnp.where(lane < LANES // 2, vert_swap, q_odd) == 1

    for copy in early:
        copy.wait()
    first = remote(out1, face1, send1.at[0], recv1.at[0], (vertical, q))
    for k in range(4):
        for c in range(2):
            left = map_ref[c, pl.ds(starts[k], side), :LANES]
            right = map_ref[c, pl.ds(starts[k], side), LANES:]
            m0[c, k * side : (k + 1) * side, :LANES] = jnp.where(cross, right, left)
            m0[c, k * side : (k + 1) * side, LANES:] = jnp.where(cross, left, right)
        if k == 0:
            out1[...] = m0[:, :side].astype(WIRE)
            first.start()

    for exists, _, _, copy in halos:

        @pl.when(exists)
        def _():
            copy().start()

    pad = 8
    locals_[0].wait()

    def apart(k, carry):
        slot = lax.rem(k, UNROLL)
        plain[slot] = guess_v[k].astype(F32)
        for c in range(2):
            field[c, k + 1, pad : pad + length] = plain[slot, pl.ds(c, length, 2), :]
        return carry

    lax.fori_loop(0, length, apart, 0, unroll=UNROLL)
    coef_v[...] = jnp.zeros_like(coef_v)
    coef_v[:length, :length] = coef_ref[...]
    coef_t = jnp.transpose(coef_v[...])[:length]
    coef_v[:length] = coef_t
    first.wait()
    mine = rows([m0[0, :side], m0[1, :side]])
    theirs = rows([face1[0].astype(F32), face1[1].astype(F32)])
    across = embed_low(theirs[:side, :LANES], theirs[side:, :LANES])
    cross1[0] = across
    product = dot3(across, mine)
    turned = tile(product, 0)
    inv = inverse(embed_low(turned[:side], turned[side:]), pow_ref, inv_ref)
    cross1[1] = inv
    wave = dot3(inv, cols([
        jnp.where(low_lanes(turned.shape), half_roll(turned), -tile(theirs, 0)),
        tile(product, 1),
        -tile(theirs, 1),
    ]))
    rest = m0[0, side:], m0[1, side:]
    gain = dot3(embed_low(tile(rest[0], 0), tile(rest[1], 0)), wave)
    count = 3 * side
    for c in range(2):
        part = gain[c * count : (c + 1) * count]
        first_tile = tile(rest[c], 0)
        m1[c, :, :LANES] = tile(part, 0) + jnp.where(
            low_lanes(first_tile.shape), half_roll(first_tile), 0.0
        )
        m1[c, :, LANES : 2 * LANES] = tile(part, 1) + tile(rest[c], 1)
        m1[c, :, 2 * LANES :] = tile(part, 2)
    out2[...] = m1[:, :side].astype(WIRE)

    def exchange(src, face, kind):
        return (
            remote(src, face.at[0], send2.at[kind, 0], recv2.at[kind, 0], (vertical, q)),
            remote(src, face.at[1], send2.at[kind, 1], recv2.at[kind, 1], (p, beside)),
            remote(face.at[0], face.at[2], send2.at[kind, 2], recv2.at[kind, 2], (p, beside)),
        )

    maps2 = exchange(out2, face2, 0)
    maps2[0].start()
    maps2[1].start()

    for num, (exists, arrives, _, copy) in enumerate(halos):

        @pl.when(arrives)
        def _():
            copy().wait_recv()
            if num < 2:
                plain[0] = edge_v[num].astype(F32)
                for c in range(2):
                    field[c, (0, length + 1)[num], pad : pad + length] = plain[0, pl.ds(c, length, 2), :]
            else:
                strip = beside_v[num - 2].astype(F32)
                at = (pad - 1, pad + length)[num - 2]
                for c in range(2):
                    field[c, 1 : length + 1, at : at + 1] = strip[:, c : c + 1]

        @pl.when(jnp.logical_not(arrives))
        def _():
            for c in range(2):
                if num < 2:
                    field[c, (0, length + 1)[num], pad : pad + length] = jnp.zeros((length, LANES), F32)
                else:
                    at = (pad - 1, pad + length)[num - 2]
                    field[c, 1 : length + 1, at : at + 1] = jnp.zeros((length, 1, LANES), F32)

    locals_[1].wait()

    def residual_row(k, carry):
        slot = lax.rem(k, UNROLL)
        plain[slot] = source_v[k].astype(F32)
        wave_term = jnp.broadcast_to(
            pltpu.roll(coef_v[:length], lax.rem(LANES - k, LANES), 1)[:, :1], (length, LANES)
        )
        diagonal_term = 4.0 - wave_term
        damp = wave_term * DAMPING
        center = [field[c, k + 1, pad : pad + length] for c in range(2)]
        around = [
            field[c, k + 2, pad : pad + length]
            + field[c, k, pad : pad + length]
            + field[c, k + 1, pad + 1 : pad + 1 + length]
            + field[c, k + 1, pad - 1 : pad - 1 + length]
            for c in range(2)
        ]
        real_part = diagonal_term * center[0] + damp * center[1] - around[0]
        imag_part = diagonal_term * center[1] - damp * center[0] - around[1]
        real = (plain[slot, pl.ds(0, length, 2), :] - real_part).astype(BF16)
        imag = (plain[slot, pl.ds(1, length, 2), :] - imag_part).astype(BF16)
        at = pl.ds(pl.multiple_of(k * length, length), length)
        load_a[at, :LANES] = real
        load_a[at, LANES:] = imag
        load_b[at, :LANES] = -imag
        load_b[at, LANES:] = real
        return carry

    lax.fori_loop(0, length // 2, residual_row, 0, unroll=UNROLL)
    maps2[0].wait_recv()
    maps2[2].start()
    lax.fori_loop(length // 2, length, residual_row, 0, unroll=UNROLL)

    locals_[2].wait()
    leaf = dot1(body_v[0], load_a[...]) + dot1(body_v[1], load_b[...])
    inv_ref[...] = leaf
    for k in range(4):
        for c in range(2):
            h0[c, k * side : (k + 1) * side] = inv_ref[
                pl.ds(starts[k], side), c * LANES : (c + 1) * LANES
            ]
    first_h = remote(h0.at[:, :side], face1h, send1.at[1], recv1.at[1], (vertical, q))
    first_h.start()
    first_h.wait()
    wave = dot3(
        cross1[1],
        dot3(cross1[0], rows([h0[0, :side], h0[1, :side]])) - rows([face1h[0], face1h[1]]),
    )
    rest = m0[0, side:], m0[1, side:]
    gain = dot3(embed_low(tile(rest[0], 0), tile(rest[1], 0)), wave)
    for c in range(2):
        h1[c] = gain[c * count : (c + 1) * count] + h0[c, side:]
    data2 = exchange(h1.at[:, :side], face2h, 1)
    data2[0].start()
    data2[1].start()

    maps2[1].wait_recv()
    maps2[2].wait_recv()
    for copy in maps2:
        copy.wait_send()
    mine = rows([
        x for c in range(2) for x in (m1[c, :side], swapped_view(face2[0, c].astype(F32)))
    ])
    theirs = rows([
        x
        for c in range(2)
        for x in (face2[1, c].astype(F32), swapped_view(face2[2, c].astype(F32)))
    ])
    across = embed(theirs[: 2 * side, :LANES], theirs[2 * side :, :LANES])
    cross2[0] = across
    product = dot3(across, mine)
    turned = tile(product, 0)
    inv = inverse(embed(turned[: 2 * side], turned[2 * side :]), pow_ref, inv_ref)
    cross2[1] = inv
    wave = dot3(inv, cols([
        tile(product, 1), tile(product, 2), -tile(theirs, 1), -tile(theirs, 2),
    ]))
    rest = m1[0, side:], m1[1, side:]
    gain = dot3(embed(tile(rest[0], 0), tile(rest[1], 0)), wave)
    count2 = 2 * side
    for c in range(2):
        part = gain[c * count2 : (c + 1) * count2]
        t_own = tile(part, 0) + tile(rest[c], 1)
        t_vert = tile(part, 1) + tile(rest[c], 2)
        t_side = tile(part, 2)
        t_diag = tile(part, 3)
        own_0 = jnp.where(q_odd == 1, t_side, t_own)
        own_1 = jnp.where(q_odd == 1, t_own, t_side)
        vert_0 = jnp.where(q_odd == 1, t_diag, t_vert)
        vert_1 = jnp.where(q_odd == 1, t_vert, t_diag)
        in_0 = jnp.where(inner, own_0, vert_0)
        in_1 = jnp.where(inner, own_1, vert_1)
        out_0 = jnp.where(inner, vert_0, own_0)
        out_1 = jnp.where(inner, vert_1, own_1)
        m2[c, :, :LANES] = low_low(in_0, in_1)
        m2[c, :, LANES : 2 * LANES] = low_low(out_0, out_1)
        m2[c, :, 2 * LANES : 3 * LANES] = jnp.where(
            lower, high_high(out_1, in_1), high_high(in_1, out_1)
        )
        m2[c, :, 3 * LANES :] = jnp.where(
            lower, high_high(out_0, in_0), high_high(in_0, out_0)
        )
    out3[...] = m2[:, :side].astype(WIRE)

    def last_copies(src, face, kind):
        first_rows = src
        def send(source, box, slot, target):
            return remote(
                source, face.at[box, q_odd], send3.at[kind, slot], recv3.at[kind, slot], target
            )

        def plane(source, slot, target):
            return [
                lambda c=c: remote(
                    source(c), face.at[1, q_odd, c],
                    send3.at[kind, slot + c], recv3.at[kind, slot + c], target,
                )
                for c in range(2)
            ]

        return (
            lambda: send(src, 0, 0, (vertical, q)),
            plane(lambda c: face.at[1, q_odd, c], 2, (vertical, q)),
            plane(lambda c: first_rows.at[c], 4, (facing, q)),
            lambda: send(src, 0, 1, (p, beside)),
            lambda: send(face.at[0, q_odd], 0, 1, (p, beside)),
            plane(lambda c: face.at[1, q_odd, c], 6, (p, beside)),
        )

    def last_start(copies, src, face):
        up_own, up_other, over, side_own, side_relay, side_other = copies

        @pl.when(inner)
        def _():
            for c in range(2):
                over[c]().start()
            up_own().start()
            side_own().start()
            face[0, q_odd] = src[:, :side]

    def inner_relay(copies):
        up_own, up_other, over, side_own, side_relay, side_other = copies

        @pl.when(inner)
        def _():
            for c in range(2):
                over[c]().wait_recv()
                up_other[c]().start()
                side_other[c]().start()

    def outer_relay(copies):
        up_own, up_other, over, side_own, side_relay, side_other = copies

        @pl.when(jnp.logical_not(inner))
        def _():
            up_own().wait_recv()
            side_relay().start()
            for c in range(2):
                up_other[c]().wait_recv()
                side_other[c]().start()

    def last_wait(copies):
        up_own, up_other, over, side_own, side_relay, side_other = copies
        side_own().wait_recv()
        for c in range(2):
            side_other[c]().wait_recv()

    def last_drain(copies):
        up_own, up_other, over, side_own, side_relay, side_other = copies
        side_own().wait_send()
        for c in range(2):
            side_other[c]().wait_send()

        @pl.when(inner)
        def _():
            up_own().wait_send()
            for c in range(2):
                over[c]().wait_send()
                up_other[c]().wait_send()

    maps3 = last_copies(out3, face3, 0)
    last_start(maps3, out3, face3)

    data2[0].wait_recv()
    data2[2].start()
    data2[1].wait_recv()
    data2[2].wait_recv()
    mine = rows([x for c in range(2) for x in (h1[c, :side], face2h[0, c])])
    theirs = rows([x for c in range(2) for x in (face2h[1, c], face2h[2, c])])
    wave = dot3(cross2[1], dot3(cross2[0], mine) - theirs)
    rest = m1[0, side:], m1[1, side:]
    gain = dot3(embed(tile(rest[0], 0), tile(rest[1], 0)), wave)
    for c in range(2):
        h2[c] = gain[c * count2 : (c + 1) * count2] + h1[c, side:]
    data3 = last_copies(h2.at[:, :side], face3h, 1)
    last_start(data3, h2, face3h)
    inner_relay(maps3)
    outer_relay(maps3)
    inner_relay(data3)

    last_wait(maps3)
    mine = rows([face3[0, j, c].astype(F32) for c in range(2) for j in range(2)])
    theirs = rows([face3[1, j, c].astype(F32) for c in range(2) for j in range(2)])
    across = embed(theirs[: 2 * side, :LANES], theirs[2 * side :, :LANES])
    product = dotw(across, mine)
    turned = tile(product, 0)
    inv = inverse(embed(turned[: 2 * side], turned[2 * side :]), pow_ref, inv_ref)
    begin = pl.multiple_of(inner_num * side, side)
    rest = m2[0, pl.ds(begin, side)], m2[1, pl.ds(begin, side)]
    out_gain = dotw(embed(tile(rest[0], 0), tile(rest[1], 0)), inv)
    cross3[0] = across
    cross3[1, : 2 * side] = out_gain
    gain = dotw(out_gain, cols(
        [tile(product, k) for k in range(1, 4)] + [-tile(theirs, k) for k in range(1, 4)]
    ))
    for c in range(2):
        part = gain[c * side : (c + 1) * side]
        own = [tile(part, k) + tile(rest[c], k + 1) for k in range(3)]
        other = [tile(part, k + 3) for k in range(3)]
        low = [jnp.where(lower, a, b) for a, b in zip(own, other)]
        up = [jnp.where(lower, b, a) for a, b in zip(own, other)]
        for k, value in enumerate([low[0], low[1], low[2], up[1], up[0], up[2]]):
            top_ref[c, :, k * LANES : (k + 1) * LANES] = value
    outer_relay(data3)
    last_wait(data3)
    mine = rows([face3h[0, j, c] for c in range(2) for j in range(2)])
    theirs = rows([face3h[1, j, c] for c in range(2) for j in range(2)])
    gain = dot3(cross3[1, : 2 * side], dot3(cross3[0], mine) - theirs)
    for c in range(2):
        top_out_ref[c] = gain[c * side : (c + 1) * side] + h2[c, pl.ds(begin, side)]
    for copy in data2:
        copy.wait_send()
    last_drain(maps3)
    last_drain(data3)
    for exists, _, _, copy in halos:

        @pl.when(exists)
        def _():
            copy().wait_send()


def place_kernel(map_ref, out_ref, top_ref, top_out_ref):
    top_ref[...] = map_ref[...]
    top_out_ref[...] = out_ref[...]


def on_device(source, guess, coefficient, leaf_map, body_map):
    length, width, _, rhs = guess.shape
    order = leaf_map.shape[3]
    side = order // 4
    vmem = pl.BlockSpec(memory_space=pltpu.VMEM)
    hbm = pl.BlockSpec(memory_space=pl.ANY)
    dma = pltpu.SemaphoreType.DMA
    rows_of = lambda x: x.reshape(length, 2 * width, rhs)
    own_map, own_out = pl.pallas_call(
        tree_kernel,
        name="build_tree",
        out_shape=(
            jax.ShapeDtypeStruct((2, side, 12 * side), F32),
            jax.ShapeDtypeStruct((2, side, rhs), F32),
        ),
        in_specs=[hbm] * 6,
        out_specs=(vmem, vmem),
        scratch_shapes=[
            pltpu.VMEM((length, 2 * width, rhs), BF16),
            pltpu.VMEM((length, 2 * width, rhs), BF16),
            pltpu.VMEM((2, order, length * width), BF16),
            pltpu.VMEM((length, width), F32),
            pltpu.VMEM((2, order, order), F32),
            pltpu.VMEM((2, 2 * width, rhs), BF16),
            pltpu.VMEM((2, length, 2, rhs), BF16),
            pltpu.VMEM((LANES, LANES), F32),
            pltpu.VMEM((UNROLL, 2 * width, rhs), F32),
            pltpu.VMEM((2, length + 2, width + 16, rhs), F32),
            pltpu.VMEM((length * width, 2 * rhs), BF16),
            pltpu.VMEM((length * width, 2 * rhs), BF16),
            pltpu.VMEM((2, order, order), F32),
            pltpu.VMEM((2, order, rhs), F32),
            pltpu.VMEM((2, 3 * side, 6 * side), F32),
            pltpu.VMEM((2, 3 * side, rhs), F32),
            pltpu.VMEM((2, 2 * side, 8 * side), F32),
            pltpu.VMEM((2, 2 * side, rhs), F32),
            pltpu.VMEM((2, side, order), WIRE),
            pltpu.VMEM((2, side, 6 * side), WIRE),
            pltpu.VMEM((2, side, 8 * side), WIRE),
            pltpu.VMEM((2, side, order), WIRE),
            pltpu.VMEM((2, side, rhs), F32),
            pltpu.VMEM((3, 2, side, 6 * side), WIRE),
            pltpu.VMEM((3, 2, side, rhs), F32),
            pltpu.VMEM((2, 2, 2, side, 8 * side), WIRE),
            pltpu.VMEM((2, 2, 2, side, rhs), F32),
            pltpu.VMEM((order, order), BF16),
            pltpu.VMEM((order, order), F32),
            pltpu.VMEM((2, 2 * side, 2 * side), F32),
            pltpu.VMEM((2, order, order), F32),
            pltpu.VMEM((2, order, order), F32),
            dma((5,)), dma((4,)), dma((4,)), dma((2,)), dma((2,)),
            dma((2, 3)), dma((2, 3)), dma((2, 8)), dma((2, 8)),
        ],
        compiler_params=pltpu.CompilerParams(
            collective_id=0, has_side_effects=True, vmem_limit_bytes=56 * 1024 * 1024
        ),
    )(guess, rows_of(guess), rows_of(source), coefficient, leaf_map[0, 0], body_map[0, 0])
    own_map, own_out = pl.pallas_call(
        place_kernel,
        name="place",
        out_shape=(
            jax.ShapeDtypeStruct(own_map.shape, F32),
            jax.ShapeDtypeStruct(own_out.shape, F32),
        ),
        in_specs=[vmem, vmem],
        out_specs=(vmem, vmem),
    )(own_map, own_out)
    return (own_map[None, None], own_out[None, None])


def solution(mesh):
    placed = (
        P("tx", "ty", None, None),
        P("tx", "ty", None, None),
        P("tx", "ty"),
        P("tx", "ty", None, None, None),
        P("tx", "ty", None, None, None),
    )
    return jax.shard_map(
        on_device,
        mesh=mesh,
        in_specs=placed,
        out_specs=(P("tx", "ty", None, None, None), P("tx", "ty", None, None, None)),
        check_vma=False,
    )
```
